32 devices in a mesh: sec: 2 (over x), col: 2 (over y), elem: 8 (over z, core).
Axes of the slice: x: 2, y: 2, z: 4, core: 2. Of those that a mesh axis runs over, the one named last changes fastest.
Arguments:
- probes: float32 [64, 48, 256], P('col', 'elem'), may hold values from -6 to 6
- jacobian: float32 [2, 48, 7, 256, 256], P('sec', 'elem'), may hold values from -0.0625 to 0.0625
- neighbors: int32 [48, 7], P('elem'), may hold values from 0 to 47, as said below
- stations: int32 [512], P('elem'), may hold values from 0 to 47, as said below
- obs_weights: float32 [512, 256], P('elem'), may hold values from -0.75 to 0.75
Outputs:
- hess_probes: float32 [64, 48, 256], P('col', 'elem', 'sec')
- gram: float32 [64, 64], P('col')
The draws below stay inside these ranges and needn't reach their ends.
Inputs may be any that keep to these rules, and one draw needn't show every extreme that they name: `neighbors`: row e lists the 7 elements e - 3 to e + 3, taken modulo 48, each once, in an order drawn for each row. Station i lies in one of the 6 elements from (i // 64) * 6 on; every element holds one or more stations.
All inputs are finite; a program needn't handle non-finite values.
Results may differ from the reference program's by a relative error of at most 0.0001.
Values sent between devices are 32-bit elements; how exact they have to be, the bound alone decides.
A program may use at most 64 MiB of HBM per device.

```python
from functools import partial
import jax
import jax.numpy as jnp
from jax import lax

ORDER = 256
NBRS = 7
EL_DEV = 6
STAT_DEV = 64
STEPS = 2
SECS = 2
ELEMS = 48
COLS = 64
STATIONS = 512


def draw_neighbors(key, part):
    element_ids = jnp.arange(ELEMS, dtype=jnp.int32)
    row_keys = jax.random.split(jax.random.fold_in(key, 11), ELEMS)
    shuffle = partial(jax.random.permutation, x=NBRS)
    orders = jax.vmap(shuffle)(row_keys).astype(jnp.int32)
    radius = (NBRS - 1) // 2
    return ((element_ids[:, None] + orders - radius) % ELEMS).astype(jnp.int32)


def draw_stations(key, part):
    positions = jnp.arange(STATIONS, dtype=jnp.int32)
    block_ids = positions // STAT_DEV
    in_block = positions % STAT_DEV
    key_first, key_second = jax.random.split(jax.random.fold_in(key, 23))
    offsets = jax.random.randint(key_first, (STATIONS // STAT_DEV,), 0, EL_DEV).astype(jnp.int32)
    extras = jax.random.randint(key_second, (STATIONS,), 0, EL_DEV).astype(jnp.int32)
    within = jnp.where(in_block < EL_DEV, (in_block + offsets[block_ids]) % EL_DEV, extras)
    return (block_ids * EL_DEV + within).astype(jnp.int32)


def levels(own_key, shape, cuts, smallest, top_value):
    loudness = 1.0
    for dim, blocks in cuts:
        draws = jax.random.uniform(jax.random.fold_in(jax.random.fold_in(own_key, 6), dim), (blocks,), jnp.float32, smallest / len(cuts), top_value / len(cuts))
        loudness = loudness * jnp.repeat(jnp.exp(draws), shape[dim] // blocks).reshape((-1,) + (1,) * (len(shape) - 1 - dim))
    return loudness


def gaussian(own_key, dims, scale, reach, pieces=(), held_as=jnp.bfloat16):
    entries = scale * jax.random.normal(own_key, dims, jnp.float32)
    if pieces:
        entries = entries * levels(own_key, dims, pieces, -0.22, 0.18)
    return jnp.clip(entries, -reach, reach).astype(held_as)


def setup_inputs(seed: int = 0) -> dict:
    key_list = jax.random.split(jax.random.key(seed), 6)
    probes = gaussian(key_list[0], (COLS, ELEMS, ORDER), 1.0, 6.0, ((0, 2), (1, 8)), jnp.float32)
    jacobian = gaussian(key_list[1], (SECS, ELEMS, NBRS, ORDER, ORDER), (4 * NBRS * ORDER) ** -0.5, 0.0625, ((0, 2), (1, 8)), jnp.float32)
    neighbors = draw_neighbors(jax.random.fold_in(key_list[5], 71), 0)
    stations = draw_stations(jax.random.fold_in(key_list[5], 71), 0)
    obs_weights = gaussian(key_list[4], (STATIONS, ORDER), (ORDER // 4) ** -0.5, 0.75, ((0, 8),), jnp.float32)
    return {"probes": probes, "jacobian": jacobian, "neighbors": neighbors, "stations": stations, "obs_weights": obs_weights}


PRECISE = lax.Precision.HIGHEST


def tangent(vector, blocks, neighbors):
    gathered = jnp.take(vector, neighbors, axis=1)
    return vector + jnp.einsum("cekI,ekJI->ceJ", gathered, blocks, precision=PRECISE)


def adjoint_step(vector, blocks, neighbors):
    products = jnp.einsum("ceJ,ekJI->cekI", vector, blocks, precision=PRECISE)
    flattened = products.reshape(products.shape[0], -1, products.shape[-1])
    returned = jnp.zeros_like(vector).at[:, neighbors.reshape(-1)].add(flattened)
    return vector + returned


def observe(vector, stations, obs_weights):
    sampled = jnp.take(vector, stations, axis=1)
    readings = jnp.einsum("csI,sI->cs", sampled, obs_weights, precision=PRECISE)
    weighted = readings[:, :, None] * obs_weights[None, :, :]
    return jnp.zeros_like(vector).at[:, stations].add(weighted)


def reference(probes, jacobian, neighbors, stations, obs_weights):
    states = []
    current = probes
    for section in range(SECS):
        for repeat in range(STEPS):
            current = tangent(current, jacobian[section], neighbors)
        states.append(current)
    adjoint = observe(states[-1], stations, obs_weights)
    for section in range(SECS - 1, -1, -1):
        for repeat in range(STEPS):
            adjoint = adjoint_step(adjoint, jacobian[section], neighbors)
        if section > 0:
            adjoint = adjoint + observe(states[section - 1], stations, obs_weights)
    flat_probes = probes.reshape(COLS, -1)
    flat_hess = adjoint.reshape(COLS, -1)
    gram = jnp.einsum("ax,bx->ab", flat_probes, flat_hess, precision=PRECISE) / (ELEMS * ORDER)
    return adjoint, gram
```

```python
import functools
import math

import jax
import jax.numpy as jnp
from jax import lax
from jax.experimental import pallas as pl
from jax.experimental.pallas import tpu as pltpu
from jax.sharding import PartitionSpec as P

STEPS = 2
MESH = pl.DeviceIdType.MESH
F32 = jnp.float32
BF16 = jnp.bfloat16
LANES = 128


def halves(value):
    high = value.astype(BF16)
    low = (value - high.astype(F32)).astype(BF16)
    return high, low


def product(a, b, transposed):
    dims = (((1,), (1 if transposed else 0,)), ((), ()))
    return lax.dot_general(a, b, dims, preferred_element_type=F32)


def product3(stack, high, low, transposed):
    rows = stack.shape[0] // 2
    first = product(stack, high, transposed)
    second = product(stack[:rows], low, transposed)
    return first[:rows] + (first[rows:] + second)


def kernel(
    sizes,
    neighbors,
    stations,
    probes_hbm,
    jacobian_hbm,
    weights_hbm,
    hess_ref,
    gram_ref,
    *scratch,
):
    cols, elems, order, nbrs, stats, n_elem, n_col = sizes
    radius = (nbrs - 1) // 2
    width = radius * order
    half = order // 2
    jac_f32 = scratch[:elems]
    jac_high = scratch[elems : 2 * elems]
    jac_low = scratch[2 * elems : 3 * elems]
    (
        probes_ref, weights_ref, state, state_in, field, from_left, from_right,
        adjoint, adjoint_in, observed, out_left, out_right, back_left, back_right,
        readings, partial, partial_in, upper, upper_in,
        load_sem, send_sem, recv_sem,
    ) = scratch[3 * elems :]
    section = lax.axis_index("sec")
    column = lax.axis_index("col")
    block = lax.axis_index("elem")
    left = lax.rem(block + n_elem - 1, n_elem)
    right = lax.rem(block + 1, n_elem)
    first_elem = block * elems
    elem_total = elems * n_elem
    rounds = int(math.log2(n_elem))

    probe_load = pltpu.make_async_copy(probes_hbm, probes_ref, load_sem.at[elems])
    probe_load.start()
    jac_loads = [
        pltpu.make_async_copy(jacobian_hbm.at[0, e], jac_f32[e], load_sem.at[e])
        for e in range(elems)
    ]
    for load in jac_loads:
        load.start()
    weights_load = pltpu.make_async_copy(
        weights_hbm, weights_ref.at[pl.ds(0, stats)], load_sem.at[elems + 1]
    )
    weights_load.start()

    barrier = pltpu.get_barrier_semaphore()
    partners = [{"elem": left}, {"elem": right}, {"sec": 1 - section}]
    partners += [{"col": lax.rem(column + j, n_col)} for j in range(1, n_col)]
    flips = []
    for r in range(rounds):
        bit = 1 << r
        upper_bit = lax.rem(block // bit, 2)
        flips.append({"elem": block + bit - 2 * bit * upper_bit})
    for partner in partners + flips:
        pl.semaphore_signal(barrier, inc=1, device_id=partner, device_id_type=MESH)
    pl.semaphore_wait(barrier, len(partners) + len(flips))

    def remote(src, dst, index, target):
        return pltpu.make_async_remote_copy(
            src_ref=src, dst_ref=dst, send_sem=send_sem.at[index],
            recv_sem=recv_sem.at[index], device_id=target, device_id_type=MESH,
        )

    FORWARD, BACKWARD, UPPER, GRAM, READ = (4 * STEPS + i for i in range(5))
    FLIP = READ + n_col - 1

    probe_load.wait()

    @pl.when(section == 0)
    def _():
        for e in range(elems):
            state[0, :, e * order : (e + 1) * order] = probes_ref[:, e, :]

    forward = remote(state.at[STEPS], state_in, FORWARD, {"sec": 1 - section})

    def halo_copies(t):
        return (
            remote(state.at[t, :, pl.ds(0, width)], from_right.at[t], 2 * t, {"elem": left}),
            remote(
                state.at[t, :, pl.ds(elems * order - width, width)],
                from_left.at[t], 2 * t + 1, {"elem": right},
            ),
        )

    @pl.when(section == 0)
    def _():
        for copy in halo_copies(0):
            copy.start()

    for e in range(elems):
        jac_loads[e].wait()

        def split_one(d, carry, e=e):
            target = lax.rem(first_elem + e + d - radius + elem_total, elem_total)
            slot = jnp.int32(0)
            for k in range(1, nbrs):
                slot = jnp.where(neighbors[e, k] == target, jnp.int32(k), slot)
            high, low = halves(jac_f32[e][slot])
            lanes = pl.ds(pl.multiple_of(d * order, order), order)
            jac_high[e][:, lanes] = high
            jac_low[e][:, lanes] = low
            return carry

        lax.fori_loop(0, nbrs, split_one, 0)

    weights_load.wait()
    weights_ref[stats:, :] = jnp.zeros((weights_ref.shape[0] - stats, order), F32)
    weights_high, weights_low = halves(weights_ref[...])
    lane_ids = lax.broadcasted_iota(jnp.int32, (cols, LANES), 1)
    station_row = jnp.full((cols, LANES), -1, jnp.int32)
    for i in range(stats):
        station_row = jnp.where(lane_ids == i, stations[i], station_row)

    @pl.when(section == 1)
    def _():
        forward.wait_recv()
        state[0] = state_in[...]
        for copy in halo_copies(0):
            copy.start()

    def put_field(start, value):
        high, low = halves(value)
        field[:cols, start : start + value.shape[1]] = high
        field[cols:, start : start + value.shape[1]] = low

    def blocks(ref, begin, end):
        return ref[:, begin * order : end * order]

    def tangent(t, carry):
        to_left, to_right = halo_copies(t)

        @pl.when(t > 0)
        def _():
            to_left.start()
            to_right.start()

        put_field(width, state[t])
        for e in range(elems):
            low, high = max(e, radius), min(e + nbrs, radius + elems)
            added = product3(
                blocks(field, low, high), blocks(jac_high[e], low - e, high - e),
                blocks(jac_low[e], low - e, high - e), True,
            )
            here = slice(e * order, (e + 1) * order)
            state[t + 1, :, here] = state[t, :, here] + added
        to_left.wait_recv()
        to_right.wait_recv()
        put_field(0, from_left[t])
        put_field(width + elems * order, from_right[t])
        for e in range(elems):
            here = slice(e * order, (e + 1) * order)
            spans = []
            if e < radius:
                spans.append((e, radius))
            if e + nbrs > radius + elems:
                spans.append((radius + elems, e + nbrs))
            total = state[t + 1, :, here]
            for low, high in spans:
                total = total + product3(
                    blocks(field, low, high), blocks(jac_high[e], low - e, high - e),
                    blocks(jac_low[e], low - e, high - e), True,
                )
            state[t + 1, :, here] = total
        to_left.wait_send()
        to_right.wait_send()
        return carry

    lax.fori_loop(0, STEPS, tangent, 0)

    @pl.when(section == 0)
    def _():
        forward.start()

    reading = jnp.zeros((cols, LANES), F32)
    for e in range(elems):
        here = slice(e * order, (e + 1) * order)
        stack = jnp.concatenate(halves(state[STEPS, :, here]), axis=0)
        read = product3(stack, weights_high, weights_low, True)
        read = jnp.where(station_row == first_elem + e, read, 0.0)
        reading = reading + read
        stack = jnp.concatenate(halves(read), axis=0)
        observed[:, here] = product3(stack, weights_high, weights_low, False)
    for slot in range(n_col, readings.shape[0]):
        readings[slot] = jnp.zeros((cols, LANES), F32)
    readings[column] = reading
    read_copies = [
        remote(
            readings.at[column], readings.at[column], READ + j - 1,
            {"col": lax.rem(column + j, n_col)},
        )
        for j in range(1, n_col)
    ]
    for copy in read_copies:
        copy.start()
    gram_copy = remote(partial.at[rounds], partial_in.at[rounds], GRAM, {"sec": 1 - section})

    def project():
        for copy in read_copies:
            copy.wait_recv()
        everyone = readings[...].reshape(readings.shape[0] * cols, LANES)
        high, low = halves(everyone)
        stack = jnp.concatenate(halves(readings[column]), axis=0)
        partial[0] = product3(stack, high, low, True)
        for r in range(rounds):
            copy = remote(partial.at[r], partial_in.at[r], FLIP + r, flips[r])
            copy.start()
            copy.wait_recv()
            partial[r + 1] = partial[r] + partial_in[r]
            copy.wait_send()
        gram_copy.start()

    backward = remote(adjoint.at[STEPS], adjoint_in, BACKWARD, {"sec": 1 - section})

    @pl.when(section == 0)
    def _():
        project()
        backward.wait_recv()
        adjoint[0] = adjoint_in[...] + observed[...]

    @pl.when(section == 1)
    def _():
        adjoint[0] = observed[...]

    def adjoint_step(t, carry):
        put_field(0, adjoint[t])
        parts = [field[:, e * order : (e + 1) * order] for e in range(elems)]

        def term(e, low, high):
            return product3(
                parts[e], blocks(jac_high[e], low - e, high - e),
                blocks(jac_low[e], low - e, high - e), False,
            )

        out_left[t] = term(0, 0, radius)
        for e in range(1, radius):
            out_left[t, :, e * order : width] = out_left[t, :, e * order : width] + term(e, e, radius)
        edge = radius + elems
        out_right[t] = term(elems - 1, edge, edge + radius)
        for e in range(elems - radius, elems - 1):
            size = (e + nbrs - edge) * order
            out_right[t, :, :size] = out_right[t, :, :size] + term(e, edge, e + nbrs)
        to_left = remote(out_left.at[t], back_right.at[t], 2 * STEPS + 2 * t, {"elem": left})
        to_right = remote(out_right.at[t], back_left.at[t], 2 * STEPS + 2 * t + 1, {"elem": right})
        to_left.start()
        to_right.start()
        adjoint[t + 1] = adjoint[t]
        for e in range(elems):
            low, high = max(e, radius), min(e + nbrs, edge)
            here = slice((low - radius) * order, (high - radius) * order)
            adjoint[t + 1, :, here] = adjoint[t + 1, :, here] + term(e, low, high)
        to_left.wait_recv()
        to_right.wait_recv()
        adjoint[t + 1, :, :width] = adjoint[t + 1, :, :width] + back_left[t]
        tail = slice(elems * order - width, elems * order)
        adjoint[t + 1, :, tail] = adjoint[t + 1, :, tail] + back_right[t]
        to_left.wait_send()
        to_right.wait_send()
        return carry

    lax.fori_loop(0, STEPS, adjoint_step, 0)

    up = remote(upper, upper_in, UPPER, {"sec": 1 - section})

    @pl.when(section == 0)
    def _():
        for e in range(elems):
            upper[e] = adjoint[STEPS, :, e * order + half : (e + 1) * order]
        up.start()
        for e in range(elems):
            hess_ref[e] = adjoint[STEPS, :, e * order : e * order + half]

    @pl.when(section == 1)
    def _():
        backward.start()
        project()

    gram_copy.wait_recv()
    scale = 1.0 / (elem_total * order)
    gram_ref[...] = (partial[rounds] + partial_in[rounds]) * scale

    @pl.when(section == 0)
    def _():
        up.wait_send()
        forward.wait_send()

    @pl.when(section == 1)
    def _():
        up.wait_recv()
        hess_ref[...] = upper_in[...]
        backward.wait_send()

    gram_copy.wait_send()
    for copy in read_copies:
        copy.wait_send()


def per_device(n_elem, n_col, probes, jacobian, neighbors, stations, obs_weights):
    cols, elems, order = probes.shape
    nbrs = neighbors.shape[1]
    stats = stations.shape[0]
    radius = (nbrs - 1) // 2
    rounds = int(math.log2(n_elem))
    slots = max(n_col, LANES // cols)
    sizes = (cols, elems, order, nbrs, stats, n_elem, n_col)
    full, width = elems * order, radius * order
    copies = 4 * STEPS + 4 + (n_col - 1) + rounds
    scratch = [pltpu.VMEM((nbrs, order, order), F32)] * elems
    scratch += [pltpu.VMEM((order, nbrs * order), BF16)] * (2 * elems)
    scratch += [
        pltpu.VMEM((cols, elems, order), F32),
        pltpu.VMEM((LANES, order), F32),
        pltpu.VMEM((STEPS + 1, cols, full), F32),
        pltpu.VMEM((cols, full), F32),
        pltpu.VMEM((2 * cols, full + 2 * width), BF16),
        pltpu.VMEM((STEPS, cols, width), F32),
        pltpu.VMEM((STEPS, cols, width), F32),
        pltpu.VMEM((STEPS + 1, cols, full), F32),
        pltpu.VMEM((cols, full), F32),
        pltpu.VMEM((cols, full), F32),
        pltpu.VMEM((STEPS, cols, width), F32),
        pltpu.VMEM((STEPS, cols, width), F32),
        pltpu.VMEM((STEPS, cols, width), F32),
        pltpu.VMEM((STEPS, cols, width), F32),
        pltpu.VMEM((slots, cols, LANES), F32),
        pltpu.VMEM((rounds + 1, cols, slots * cols), F32),
        pltpu.VMEM((rounds + 1, cols, slots * cols), F32),
        pltpu.VMEM((elems, cols, order // 2), F32),
        pltpu.VMEM((elems, cols, order // 2), F32),
        pltpu.SemaphoreType.DMA((elems + 2,)),
        pltpu.SemaphoreType.DMA((copies,)),
        pltpu.SemaphoreType.DMA((copies,)),
    ]
    smem = pl.BlockSpec(memory_space=pltpu.SMEM)
    anywhere = pl.BlockSpec(memory_space=pl.ANY)
    vmem = pl.BlockSpec(memory_space=pltpu.VMEM)
    hess, gram = pl.pallas_call(
        functools.partial(kernel, sizes),
        out_shape=(
            jax.ShapeDtypeStruct((elems, cols, order // 2), F32),
            jax.ShapeDtypeStruct((cols, slots * cols), F32),
        ),
        in_specs=[smem, smem, anywhere, anywhere, anywhere],
        out_specs=(vmem, vmem),
        scratch_shapes=scratch,
        compiler_params=pltpu.CompilerParams(
            collective_id=0, has_side_effects=True, vmem_limit_bytes=56 * 1024 * 1024
        ),
    )(neighbors, stations, probes, jacobian, obs_weights)
    return hess.transpose(1, 0, 2), gram[:, : n_col * cols]


def solution(mesh):
    in_specs = (
        P("col", "elem", None),
        P("sec", "elem", None, None, None),
        P("elem", None),
        P("elem"),
        P("elem", None),
    )
    out_specs = (P("col", "elem", "sec"), P("col", None))
    body = functools.partial(per_device, mesh.shape["elem"], mesh.shape["col"])
    return jax.shard_map(
        body, mesh=mesh, in_specs=in_specs, out_specs=out_specs, check_vma=False
    )
```

```python
import functools
import math

import jax
import jax.numpy as jnp
from jax import lax
from jax.experimental import pallas as pl
from jax.experimental.pallas import tpu as pltpu
from jax.sharding import PartitionSpec as P

STEPS = 2
MESH = pl.DeviceIdType.MESH
F32 = jnp.float32
BF16 = jnp.bfloat16
LANES = 128


def halves(value):
    high = value.astype(BF16)
    low = (value - high.astype(F32)).astype(BF16)
    return high, low


def product(a, b, transposed):
    dims = (((1,), (1 if transposed else 0,)), ((), ()))
    return lax.dot_general(a, b, dims, preferred_element_type=F32)


def product3(stack, high, low, transposed):
    rows = stack.shape[0] // 2
    first = product(stack, high, transposed)
    second = product(stack[:rows], low, transposed)
    return first[:rows] + (first[rows:] + second)


def kernel(
    sizes,
    neighbors,
    stations,
    probes_hbm,
    jacobian_hbm,
    weights_hbm,
    hess_ref,
    gram_ref,
    *scratch,
):
    cols, elems, order, nbrs, stats, n_elem, n_col = sizes
    radius = (nbrs - 1) // 2
    width = radius * order
    half = order // 2
    jac_f32 = scratch[:elems]
    jac_high = scratch[elems : 2 * elems]
    jac_low = scratch[2 * elems : 3 * elems]
    (
        probes_ref, weights_ref, state, field, halo_left, halo_right,
        adjoint, adjoint_in, observed, out_left, out_right, back_left, back_right,
        back_across, readings, partial, partial_in, upper, upper_in,
        load_sem, send_sem, recv_sem,
    ) = scratch[3 * elems :]
    section = lax.axis_index("sec")
    column = lax.axis_index("col")
    block = lax.axis_index("elem")
    left = lax.rem(block + n_elem - 1, n_elem)
    right = lax.rem(block + 1, n_elem)
    even = lax.rem(block, 2) == 0
    far = jnp.where(even, left, right)
    other = 1 - section
    first_elem = block * elems
    elem_total = elems * n_elem
    rounds = int(math.log2(n_elem))
    edge = radius + elems
    full = elems * order
    last = STEPS - 1
    LEFT, RIGHT = 0, 1
    neighbour = (left, right)
    halo_in = (halo_left, halo_right)
    out = (out_left, out_right)
    back = (back_left, back_right)
    own = (slice(0, width), slice(full - width, full))
    own_ds = (pl.ds(0, width), pl.ds(full - width, width))
    own_elems = (range(0, radius), range(elems - radius, elems))

    def by_parity(run):
        @pl.when(even)
        def _():
            run(RIGHT, LEFT)

        @pl.when(jnp.logical_not(even))
        def _():
            run(LEFT, RIGHT)

    probe_load = pltpu.make_async_copy(probes_hbm, probes_ref, load_sem.at[elems])
    probe_load.start()
    jac_loads = [
        pltpu.make_async_copy(jacobian_hbm.at[0, e], jac_f32[e], load_sem.at[e])
        for e in range(elems)
    ]
    for load in jac_loads:
        load.start()
    weights_load = pltpu.make_async_copy(
        weights_hbm, weights_ref.at[pl.ds(0, stats)], load_sem.at[elems + 1]
    )
    weights_load.start()

    barrier = pltpu.get_barrier_semaphore()
    partners = [{"elem": left}, {"elem": right}, {"sec": other}, {"sec": other, "elem": far}]
    partners += [{"col": lax.rem(column + j, n_col)} for j in range(1, n_col)]
    flips = []
    for r in range(rounds):
        bit = 1 << r
        upper_bit = lax.rem(block // bit, 2)
        flips.append({"elem": block + bit - 2 * bit * upper_bit})
    for partner in partners + flips:
        pl.semaphore_signal(barrier, inc=1, device_id=partner, device_id_type=MESH)

    probe_load.wait()

    @pl.when(section == 0)
    def _():
        for e in range(elems):
            state[0, :, e * order : (e + 1) * order] = probes_ref[e]

    pl.semaphore_wait(barrier, len(partners) + len(flips))

    def remote(src, dst, index, target, arrival=None):
        arrival = index if arrival is None else arrival
        return pltpu.make_async_remote_copy(
            src_ref=src, dst_ref=dst, send_sem=send_sem.at[index],
            recv_sem=recv_sem.at[arrival], device_id=target, device_id_type=MESH,
        )

    FORWARD = 4 * STEPS
    BACKWARD, UPPER = FORWARD + 2, FORWARD + 4
    ACROSS, RETURN, GRAM, READ = (FORWARD + 6 + i for i in range(4))
    FLIP = READ + n_col - 1

    def halo_copy(t, side):
        return remote(
            state.at[t, :, own_ds[side]], halo_in[1 - side].at[t], 2 * t + side,
            {"elem": neighbour[side]},
        )

    def halo_across(side):
        return remote(
            state.at[STEPS, :, own_ds[side]], halo_in[1 - side].at[0], ACROSS,
            {"sec": other, "elem": neighbour[side]}, side,
        )

    def forward(side):
        return remote(
            state.at[STEPS, :, own_ds[side]], state.at[0, :, own_ds[side]],
            FORWARD + side, {"sec": other},
        )

    def out_copy(t, side):
        return remote(
            out[side].at[t], back[1 - side].at[t], 2 * STEPS + 2 * t + side,
            {"elem": neighbour[side]},
        )

    def out_across(side):
        return remote(
            out[side].at[last], back_across, RETURN, {"sec": other, "elem": neighbour[side]}
        )

    def backward(side):
        return remote(
            adjoint.at[STEPS, :, own_ds[side]], adjoint_in.at[:, own_ds[side]],
            BACKWARD + side, {"sec": other},
        )

    def up(side):
        rows = pl.ds(own_elems[side].start, radius)
        return remote(upper.at[rows], upper_in.at[rows], UPPER + side, {"sec": other})

    @pl.when(section == 0)
    def _():
        halo_copy(0, LEFT).start()
        halo_copy(0, RIGHT).start()

    for e in range(elems):
        jac_loads[e].wait()

        def split_one(d, carry, e=e):
            target = lax.rem(first_elem + e + d - radius + elem_total, elem_total)
            slot = jnp.int32(0)
            for k in range(1, nbrs):
                slot = jnp.where(neighbors[e, k] == target, jnp.int32(k), slot)
            high, low = halves(jac_f32[e][slot])
            lanes = pl.ds(pl.multiple_of(d * order, order), order)
            jac_high[e][:, lanes] = high
            jac_low[e][:, lanes] = low
            return carry

        lax.fori_loop(0, nbrs, split_one, 0)

    weights_load.wait()
    weights_ref[stats:, :] = jnp.zeros((weights_ref.shape[0] - stats, order), F32)
    weights_high, weights_low = halves(weights_ref[...])
    lane_ids = lax.broadcasted_iota(jnp.int32, (cols, LANES), 1)
    station_row = jnp.full((cols, LANES), -1, jnp.int32)
    for i in range(stats):
        station_row = jnp.where(lane_ids == i, stations[i], station_row)

    def receive_forward(core, away):
        @pl.when(section == 1)
        def _():
            forward(core).wait_recv()
            halo_copy(0, core).start()
            forward(away).wait_recv()

    by_parity(receive_forward)

    def put_field(start, value):
        high, low = halves(value)
        field[:cols, start : start + value.shape[1]] = high
        field[cols:, start : start + value.shape[1]] = low

    def blocks(ref, begin, end):
        return ref[:, begin * order : end * order]

    def gathered(e, low, high):
        return product3(
            blocks(field, low, high), blocks(jac_high[e], low - e, high - e),
            blocks(jac_low[e], low - e, high - e), True,
        )

    def here(e):
        return slice(e * order, (e + 1) * order)

    def finish_tangent(t, side, away):
        halo_copy(t, 1 - side).wait_recv()
        put_field(0 if side == LEFT else width + full, halo_in[side][t])
        for e in own_elems[side]:
            span = (e, radius) if side == LEFT else (edge, e + nbrs)
            state[t + 1, :, here(e)] = state[t + 1, :, here(e)] + gathered(e, *span)
        if t < last:
            halo_copy(t + 1, side).start()
        else:

            @pl.when(section == 0)
            def _():
                forward(side).start()
                if away:
                    halo_across(side).start()

    for t in range(STEPS):
        put_field(width, state[t])
        for e in range(elems):
            added = gathered(e, max(e, radius), min(e + nbrs, edge))
            state[t + 1, :, here(e)] = state[t, :, here(e)] + added

        def finish(core, away, t=t):
            finish_tangent(t, core, False)
            finish_tangent(t, away, True)

        by_parity(finish)

    reading = jnp.zeros((cols, LANES), F32)
    for e in range(elems):
        stack = jnp.concatenate(halves(state[STEPS, :, here(e)]), axis=0)
        read = product3(stack, weights_high, weights_low, True)
        read = jnp.where(station_row == first_elem + e, read, 0.0)
        reading = reading + read
        stack = jnp.concatenate(halves(read), axis=0)
        observed[:, here(e)] = product3(stack, weights_high, weights_low, False)
    for slot in range(n_col, readings.shape[0]):
        readings[slot] = jnp.zeros((cols, LANES), F32)
    readings[column] = reading
    read_copies = [
        remote(
            readings.at[column], readings.at[column], READ + j - 1,
            {"col": lax.rem(column + j, n_col)},
        )
        for j in range(1, n_col)
    ]
    for copy in read_copies:
        copy.start()
    gram_copy = remote(partial.at[rounds], partial_in.at[rounds], GRAM, {"sec": other})

    def project():
        for copy in read_copies:
            copy.wait_recv()
        everyone = readings[...].reshape(readings.shape[0] * cols, LANES)
        high, low = halves(everyone)
        stack = jnp.concatenate(halves(readings[column]), axis=0)
        partial[0] = product3(stack, high, low, True)
        for r in range(rounds):
            copy = remote(partial.at[r], partial_in.at[r], FLIP + r, flips[r])
            copy.start()
            copy.wait_recv()
            partial[r + 1] = partial[r] + partial_in[r]
            copy.wait_send()
        gram_copy.start()

    @pl.when(section == 0)
    def _():
        project()

    def spread(e, low, high):
        return product3(
            field[:, here(e)], blocks(jac_high[e], low - e, high - e),
            blocks(jac_low[e], low - e, high - e), False,
        )

    def send_out(t, side, away):
        put_field(own[side].start, adjoint[t, :, own[side]])
        ref = out[side]
        if side == LEFT:
            ref[t] = spread(0, 0, radius)
            for e in range(1, radius):
                ref[t, :, e * order :] = ref[t, :, e * order :] + spread(e, e, radius)
        else:
            ref[t] = spread(elems - 1, edge, edge + radius)
            for e in range(elems - radius, elems - 1):
                size = (e + nbrs - edge) * order
                ref[t, :, :size] = ref[t, :, :size] + spread(e, edge, e + nbrs)
        if t == last and away:

            @pl.when(section == 0)
            def _():
                out_copy(t, side).start()

            @pl.when(section == 1)
            def _():
                out_across(side).start()

        else:
            out_copy(t, side).start()

    def begin_adjoint(core, away):
        for side in (away, core):
            lanes = own[side]

            @pl.when(section == 0)
            def _():
                backward(side).wait_recv()
                total = adjoint_in[:, lanes] + observed[:, lanes]
                if side == away:
                    out_across(1 - side).wait_recv()
                    total = total + back_across[...]
                adjoint[0, :, lanes] = total

            @pl.when(section == 1)
            def _():
                adjoint[0, :, lanes] = observed[:, lanes]

            send_out(0, side, side == away)

    by_parity(begin_adjoint)

    def emit(side):
        for e in own_elems[side]:
            upper[e] = adjoint[STEPS, :, e * order + half : (e + 1) * order]
        up(side).start()
        for e in own_elems[side]:
            hess_ref[e] = adjoint[STEPS, :, e * order : e * order + half]

    def finish_adjoint(t, side, away):
        lanes = own[side]

        def add():
            out_copy(t, 1 - side).wait_recv()
            adjoint[t + 1, :, lanes] = adjoint[t + 1, :, lanes] + back[side][t]

        if t < last:
            add()
            send_out(t + 1, side, away)
        else:

            @pl.when(section == 0)
            def _():
                add()
                emit(side)

            @pl.when(section == 1)
            def _():
                if not away:
                    add()
                backward(side).start()

    for t in range(STEPS):
        adjoint[t + 1] = adjoint[t]
        for e in range(elems):
            low, high = max(e, radius), min(e + nbrs, edge)
            lanes = slice((low - radius) * order, (high - radius) * order)
            adjoint[t + 1, :, lanes] = adjoint[t + 1, :, lanes] + spread(e, low, high)

        def finish(core, away, t=t):
            if t == last:

                @pl.when(section == 1)
                def _():
                    finish_adjoint(t, away, True)
                    finish_adjoint(t, core, False)

                @pl.when(section == 0)
                def _():
                    finish_adjoint(t, core, False)
                    finish_adjoint(t, away, True)

            else:
                finish_adjoint(t, core, False)
                finish_adjoint(t, away, True)

        by_parity(finish)

    @pl.when(section == 1)
    def _():
        project()

    gram_copy.wait_recv()
    scale = 1.0 / (elem_total * order)
    gram_ref[...] = (partial[rounds] + partial_in[rounds]) * scale

    def close(core, away):
        for t in range(STEPS):
            for side in (core, away):

                @pl.when((section == 0) | (t > 0) | (side == core))
                def _():
                    halo_copy(t, side).wait_send()

                @pl.when((section == 0) | (t < last) | (side == core))
                def _():
                    out_copy(t, side).wait_send()

        @pl.when(section == 0)
        def _():
            halo_across(away).wait_send()
            for side in (core, away):
                forward(side).wait_send()
                up(side).wait_send()

        @pl.when(section == 1)
        def _():
            out_across(away).wait_send()
            for side in (core, away):
                backward(side).wait_send()
                up(side).wait_recv()
            hess_ref[...] = upper_in[...]

    by_parity(close)
    gram_copy.wait_send()
    for copy in read_copies:
        copy.wait_send()


def per_device(n_elem, n_col, probes, jacobian, neighbors, stations, obs_weights):
    cols, elems, order = probes.shape
    nbrs = neighbors.shape[1]
    stats = stations.shape[0]
    radius = (nbrs - 1) // 2
    rounds = int(math.log2(n_elem))
    slots = max(n_col, LANES // cols)
    sizes = (cols, elems, order, nbrs, stats, n_elem, n_col)
    full, width = elems * order, radius * order
    copies = 4 * STEPS + 9 + (n_col - 1) + rounds
    scratch = [pltpu.VMEM((nbrs, order, order), F32)] * elems
    scratch += [pltpu.VMEM((order, nbrs * order), BF16)] * (2 * elems)
    scratch += [
        pltpu.VMEM((elems, cols, order), F32),
        pltpu.VMEM((LANES, order), F32),
        pltpu.VMEM((STEPS + 1, cols, full), F32),
        pltpu.VMEM((2 * cols, full + 2 * width), BF16),
        pltpu.VMEM((STEPS, cols, width), F32),
        pltpu.VMEM((STEPS, cols, width), F32),
        pltpu.VMEM((STEPS + 1, cols, full), F32),
        pltpu.VMEM((cols, full), F32),
        pltpu.VMEM((cols, full), F32),
        pltpu.VMEM((STEPS, cols, width), F32),
        pltpu.VMEM((STEPS, cols, width), F32),
        pltpu.VMEM((STEPS, cols, width), F32),
        pltpu.VMEM((STEPS, cols, width), F32),
        pltpu.VMEM((cols, width), F32),
        pltpu.VMEM((slots, cols, LANES), F32),
        pltpu.VMEM((rounds + 1, cols, slots * cols), F32),
        pltpu.VMEM((rounds + 1, cols, slots * cols), F32),
        pltpu.VMEM((elems, cols, order // 2), F32),
        pltpu.VMEM((elems, cols, order // 2), F32),
        pltpu.SemaphoreType.DMA((elems + 2,)),
        pltpu.SemaphoreType.DMA((copies,)),
        pltpu.SemaphoreType.DMA((copies,)),
    ]
    smem = pl.BlockSpec(memory_space=pltpu.SMEM)
    anywhere = pl.BlockSpec(memory_space=pl.ANY)
    vmem = pl.BlockSpec(memory_space=pltpu.VMEM)
    hess, gram = pl.pallas_call(
        functools.partial(kernel, sizes),
        out_shape=(
            jax.ShapeDtypeStruct((elems, cols, order // 2), F32),
            jax.ShapeDtypeStruct((cols, slots * cols), F32),
        ),
        in_specs=[smem, smem, anywhere, anywhere, anywhere],
        out_specs=(vmem, vmem),
        scratch_shapes=scratch,
        compiler_params=pltpu.CompilerParams(
            collective_id=0, has_side_effects=True, vmem_limit_bytes=56 * 1024 * 1024
        ),
    )(neighbors, stations, probes.transpose(1, 0, 2), jacobian, obs_weights)
    return hess.transpose(1, 0, 2), gram[:, : n_col * cols]


def solution(mesh):
    in_specs = (
        P("col", "elem", None),
        P("sec", "elem", None, None, None),
        P("elem", None),
        P("elem"),
        P("elem", None),
    )
    out_specs = (P("col", "elem", "sec"), P("col", None))
    body = functools.partial(per_device, mesh.shape["elem"], mesh.shape["col"])
    return jax.shard_map(
        body, mesh=mesh, in_specs=in_specs, out_specs=out_specs, check_vma=False
    )
```

```python
import functools
import math

import jax
import jax.numpy as jnp
from jax import lax
from jax.experimental import pallas as pl
from jax.experimental.pallas import tpu as pltpu
from jax.sharding import PartitionSpec as P

STEPS = 2
MESH = pl.DeviceIdType.MESH
F32 = jnp.float32
BF16 = jnp.bfloat16
LANES = 128


def halves(value):
    high = value.astype(BF16)
    low = (value - high.astype(F32)).astype(BF16)
    return high, low


def product(a, b, transposed):
    dims = (((1,), (1 if transposed else 0,)), ((), ()))
    return lax.dot_general(a, b, dims, preferred_element_type=F32)


def product3(stack, high, low, transposed):
    rows = stack.shape[0] // 2
    first = product(stack, high, transposed)
    second = product(stack[:rows], low, transposed)
    return first[:rows] + (first[rows:] + second)


def kernel(
    sizes,
    neighbors,
    stations,
    probes_hbm,
    jacobian_hbm,
    weights_hbm,
    hess_ref,
    gram_ref,
    *scratch,
):
    cols, elems, order, nbrs, stats, n_elem, n_col = sizes
    radius = (nbrs - 1) // 2
    width = radius * order
    half = order // 2
    jac_f32 = scratch[:elems]
    jac_high = scratch[elems : 2 * elems]
    jac_low = scratch[2 * elems : 3 * elems]
    (
        probes_ref, weights_ref, state, field, halo_left, halo_right,
        adjoint, adjoint_in, observed, out_left, out_right, back_left, back_right,
        back_across, out_half, back_half, readings, partial, partial_in, upper, upper_in,
        load_sem, send_sem, recv_sem,
    ) = scratch[3 * elems :]
    section = lax.axis_index("sec")
    column = lax.axis_index("col")
    block = lax.axis_index("elem")
    left = lax.rem(block + n_elem - 1, n_elem)
    right = lax.rem(block + 1, n_elem)
    even = lax.rem(block, 2) == 0
    far = jnp.where(even, left, right)
    other = 1 - section
    first_elem = block * elems
    elem_total = elems * n_elem
    rounds = int(math.log2(n_elem))
    edge = radius + elems
    full = elems * order
    last = STEPS - 1
    LEFT, RIGHT = 0, 1
    neighbour = (left, right)
    halo_in = (halo_left, halo_right)
    out = (out_left, out_right)
    back = (back_left, back_right)
    own = (slice(0, width), slice(full - width, full))
    own_ds = (pl.ds(0, width), pl.ds(full - width, width))
    own_elems = (range(0, radius), range(elems - radius, elems))
    own_span = ((radius, 2 * radius), (edge - radius, edge))

    def by_parity(run):
        @pl.when(even)
        def _():
            run(RIGHT, LEFT)

        @pl.when(jnp.logical_not(even))
        def _():
            run(LEFT, RIGHT)

    probe_load = pltpu.make_async_copy(probes_hbm, probes_ref, load_sem.at[elems])
    probe_load.start()
    jac_loads = [
        pltpu.make_async_copy(jacobian_hbm.at[0, e], jac_f32[e], load_sem.at[e])
        for e in range(elems)
    ]
    for load in jac_loads:
        load.start()
    weights_load = pltpu.make_async_copy(
        weights_hbm, weights_ref.at[pl.ds(0, stats)], load_sem.at[elems + 1]
    )
    weights_load.start()

    barrier = pltpu.get_barrier_semaphore()
    partners = [{"elem": left}, {"elem": right}, {"sec": other}, {"sec": other, "elem": far}]
    partners += [{"col": lax.rem(column + j, n_col)} for j in range(1, n_col)]
    flips = []
    for r in range(rounds):
        bit = 1 << r
        upper_bit = lax.rem(block // bit, 2)
        flips.append({"elem": block + bit - 2 * bit * upper_bit})
    for partner in partners + flips:
        pl.semaphore_signal(barrier, inc=1, device_id=partner, device_id_type=MESH)

    probe_load.wait()

    @pl.when(section == 0)
    def _():
        for e in range(elems):
            state[0, :, e * order : (e + 1) * order] = probes_ref[e]

    pl.semaphore_wait(barrier, len(partners) + len(flips))

    def remote(src, dst, index, target, arrival=None):
        arrival = index if arrival is None else arrival
        return pltpu.make_async_remote_copy(
            src_ref=src, dst_ref=dst, send_sem=send_sem.at[index],
            recv_sem=recv_sem.at[arrival], device_id=target, device_id_type=MESH,
        )

    FORWARD = 4 * STEPS
    BACKWARD, UPPER = FORWARD + 2, FORWARD + 4
    ACROSS, RETURN, GRAM, LOWER, HIGHER, READ = (FORWARD + 6 + i for i in range(6))
    FLIP = READ + n_col - 1

    def halo_copy(t, side):
        return remote(
            state.at[t, :, own_ds[side]], halo_in[1 - side].at[t], 2 * t + side,
            {"elem": neighbour[side]},
        )

    def halo_across(side):
        return remote(
            state.at[STEPS, :, own_ds[side]], halo_in[1 - side].at[0], ACROSS,
            {"sec": other, "elem": neighbour[side]}, side,
        )

    def forward(side):
        return remote(
            state.at[STEPS, :, own_ds[side]], state.at[0, :, own_ds[side]],
            FORWARD + side, {"sec": other},
        )

    def out_copy(t, side):
        return remote(
            out[side].at[t], back[1 - side].at[t], 2 * STEPS + 2 * t + side,
            {"elem": neighbour[side]},
        )

    def out_across(side):
        return remote(
            out[side].at[last], back_across, RETURN, {"sec": other, "elem": neighbour[side]}
        )

    def backward(side):
        return remote(
            adjoint.at[STEPS, :, own_ds[side]], adjoint_in.at[:, own_ds[side]],
            BACKWARD + side, {"sec": other},
        )

    def half_copy(part, side):
        return remote(
            out_half.at[part], back_half, (LOWER, HIGHER)[part],
            {"sec": section if part == 0 else other, "elem": neighbour[side]},
        )

    def up(side):
        rows = pl.ds(own_elems[side].start, radius)
        return remote(upper.at[rows], upper_in.at[rows], UPPER + side, {"sec": other})

    @pl.when(section == 0)
    def _():
        halo_copy(0, LEFT).start()
        halo_copy(0, RIGHT).start()

    for e in range(elems):
        jac_loads[e].wait()

        def split_one(d, carry, e=e):
            target = lax.rem(first_elem + e + d - radius + elem_total, elem_total)
            slot = jnp.int32(0)
            for k in range(1, nbrs):
                slot = jnp.where(neighbors[e, k] == target, jnp.int32(k), slot)
            high, low = halves(jac_f32[e][slot])
            lanes = pl.ds(pl.multiple_of(d * order, order), order)
            jac_high[e][:, lanes] = high
            jac_low[e][:, lanes] = low
            return carry

        lax.fori_loop(0, nbrs, split_one, 0)

    weights_load.wait()
    weights_ref[stats:, :] = jnp.zeros((weights_ref.shape[0] - stats, order), F32)
    weights_high, weights_low = halves(weights_ref[...])
    lane_ids = lax.broadcasted_iota(jnp.int32, (cols, LANES), 1)
    station_row = jnp.full((cols, LANES), -1, jnp.int32)
    for i in range(stats):
        station_row = jnp.where(lane_ids == i, stations[i], station_row)

    def put_field(start, value):
        high, low = halves(value)
        field[:cols, start : start + value.shape[1]] = high
        field[cols:, start : start + value.shape[1]] = low

    def blocks(ref, begin, end):
        return ref[:, begin * order : end * order]

    def gathered(e, low, high):
        return product3(
            blocks(field, low, high), blocks(jac_high[e], low - e, high - e),
            blocks(jac_low[e], low - e, high - e), True,
        )

    def here(e):
        return slice(e * order, (e + 1) * order)

    def finish_tangent(t, side, away):
        halo_copy(t, 1 - side).wait_recv()
        put_field(0 if side == LEFT else width + full, halo_in[side][t])
        for e in own_elems[side]:
            span = (e, radius) if side == LEFT else (edge, e + nbrs)
            state[t + 1, :, here(e)] = state[t + 1, :, here(e)] + gathered(e, *span)
        if t < last:
            halo_copy(t + 1, side).start()
        else:

            @pl.when(section == 0)
            def _():
                forward(side).start()
                if away:
                    halo_across(side).start()

    def tangent(t, core, away):
        if t == 0:
            for side in (core, away):

                @pl.when(section == 1)
                def _():
                    forward(side).wait_recv()
                    if side == core:
                        halo_copy(0, core).start()

                put_field(width + own[side].start, state[0, :, own[side]])
                begin, end = own_span[side]
                for e in range(elems):
                    added = gathered(e, max(e, begin), min(e + nbrs, end))
                    if side == away:
                        added = added + (state[1, :, here(e)] + state[0, :, here(e)])
                    state[1, :, here(e)] = added
        finish_tangent(t, core, False)
        finish_tangent(t, away, True)

    for t in range(STEPS):
        if t > 0:
            put_field(width, state[t])
            for e in range(elems):
                added = gathered(e, max(e, radius), min(e + nbrs, edge))
                state[t + 1, :, here(e)] = state[t, :, here(e)] + added
        by_parity(functools.partial(tangent, t))

    reading = jnp.zeros((cols, LANES), F32)
    for e in range(elems):
        stack = jnp.concatenate(halves(state[STEPS, :, here(e)]), axis=0)
        read = product3(stack, weights_high, weights_low, True)
        read = jnp.where(station_row == first_elem + e, read, 0.0)
        reading = reading + read
        stack = jnp.concatenate(halves(read), axis=0)
        observed[:, here(e)] = product3(stack, weights_high, weights_low, False)
    for slot in range(n_col, readings.shape[0]):
        readings[slot] = jnp.zeros((cols, LANES), F32)
    readings[column] = reading
    read_copies = [
        remote(
            readings.at[column], readings.at[column], READ + j - 1,
            {"col": lax.rem(column + j, n_col)},
        )
        for j in range(1, n_col)
    ]
    for copy in read_copies:
        copy.start()
    gram_copy = remote(partial.at[rounds], partial_in.at[rounds], GRAM, {"sec": other})

    def project():
        for copy in read_copies:
            copy.wait_recv()
        everyone = readings[...].reshape(readings.shape[0] * cols, LANES)
        high, low = halves(everyone)
        stack = jnp.concatenate(halves(readings[column]), axis=0)
        partial[0] = product3(stack, high, low, True)
        for r in range(rounds):
            copy = remote(partial.at[r], partial_in.at[r], FLIP + r, flips[r])
            copy.start()
            copy.wait_recv()
            partial[r + 1] = partial[r] + partial_in[r]
            copy.wait_send()
        gram_copy.start()

    @pl.when(section == 0)
    def _():
        project()

    def spread(e, low, high):
        return product3(
            field[:, here(e)], blocks(jac_high[e], low - e, high - e),
            blocks(jac_low[e], low - e, high - e), False,
        )

    def send_out(t, side, away):
        put_field(own[side].start, adjoint[t, :, own[side]])
        ref = out[side]
        if side == LEFT:
            ref[t] = spread(0, 0, radius)
            for e in range(1, radius):
                ref[t, :, e * order :] = ref[t, :, e * order :] + spread(e, e, radius)
        else:
            ref[t] = spread(elems - 1, edge, edge + radius)
            for e in range(elems - radius, elems - 1):
                size = (e + nbrs - edge) * order
                ref[t, :, :size] = ref[t, :, :size] + spread(e, edge, e + nbrs)
        if t == last and away:

            @pl.when(section == 0)
            def _():
                for part in range(2):
                    for j in range(radius):
                        lanes = slice(j * order + part * half, j * order + (part + 1) * half)
                        out_half[part, :, j * half : (j + 1) * half] = ref[t, :, lanes]
                    half_copy(part, side).start()

            @pl.when(section == 1)
            def _():
                out_across(side).start()

        else:
            out_copy(t, side).start()

    def begin_adjoint(core, away):
        for side in (away, core):
            lanes = own[side]

            @pl.when(section == 0)
            def _():
                backward(side).wait_recv()
                total = adjoint_in[:, lanes] + observed[:, lanes]
                if side == away:
                    out_across(1 - side).wait_recv()
                    total = total + back_across[...]
                adjoint[0, :, lanes] = total

            @pl.when(section == 1)
            def _():
                adjoint[0, :, lanes] = observed[:, lanes]

            send_out(0, side, side == away)

    by_parity(begin_adjoint)

    def inner(t, side):
        begin, end = own_span[side]
        lanes = own[side]
        adjoint[t + 1, :, lanes] = adjoint[t, :, lanes]
        for e in range(elems):
            low, high = max(e, begin), min(e + nbrs, end)
            lanes = slice((low - radius) * order, (high - radius) * order)
            adjoint[t + 1, :, lanes] = adjoint[t + 1, :, lanes] + spread(e, low, high)

    def add_back(t, side):
        lanes = own[side]
        out_copy(t, 1 - side).wait_recv()
        adjoint[t + 1, :, lanes] = adjoint[t + 1, :, lanes] + back[side][t]

    def send_up(side):
        for e in own_elems[side]:
            upper[e] = adjoint[STEPS, :, e * order + half : (e + 1) * order]
        up(side).start()

    def lower_half(e):
        return adjoint[STEPS, :, e * order : e * order + half]

    def adjoint_step(t, core, away):
        if t < last:
            for side in (core, away):
                add_back(t, side)
                send_out(t + 1, side, side == away)
        else:
            inner(t, away)

            @pl.when(section == 0)
            def _():
                send_up(away)

            @pl.when(section == 1)
            def _():
                backward(away).start()

            inner(t, core)
            add_back(t, core)

            @pl.when(section == 0)
            def _():
                send_up(core)
                for e in own_elems[core]:
                    hess_ref[e] = lower_half(e)
                half_copy(0, 1 - away).wait_recv()
                for j, e in enumerate(own_elems[away]):
                    hess_ref[e] = lower_half(e) + back_half[:, j * half : (j + 1) * half]

            @pl.when(section == 1)
            def _():
                backward(core).start()

    for t in range(STEPS):
        if t < last:
            inner(t, LEFT)
            inner(t, RIGHT)
        by_parity(functools.partial(adjoint_step, t))

    @pl.when(section == 1)
    def _():
        project()

    gram_copy.wait_recv()
    scale = 1.0 / (elem_total * order)
    gram_ref[...] = (partial[rounds] + partial_in[rounds]) * scale

    def close(core, away):
        for t in range(STEPS):
            for side in (core, away):

                @pl.when((section == 0) | (t > 0) | (side == core))
                def _():
                    halo_copy(t, side).wait_send()

                if t < last or side == core:
                    out_copy(t, side).wait_send()

        @pl.when(section == 0)
        def _():
            halo_across(away).wait_send()
            for side in (core, away):
                forward(side).wait_send()
                up(side).wait_send()
            for part in range(2):
                half_copy(part, away).wait_send()

        @pl.when(section == 1)
        def _():
            out_across(away).wait_send()
            for side in (core, away):
                backward(side).wait_send()
                up(side).wait_recv()
            for e in own_elems[core]:
                hess_ref[e] = upper_in[e]
            half_copy(1, 1 - away).wait_recv()
            for j, e in enumerate(own_elems[away]):
                hess_ref[e] = upper_in[e] + back_half[:, j * half : (j + 1) * half]

    by_parity(close)
    gram_copy.wait_send()
    for copy in read_copies:
        copy.wait_send()


def hand_over(hess_ref, gram_ref, hess_out, gram_out):
    hess_out[...] = hess_ref[...]
    gram_out[...] = gram_ref[:, : gram_out.shape[1]]


def per_device(n_elem, n_col, probes, jacobian, neighbors, stations, obs_weights):
    cols, elems, order = probes.shape
    nbrs = neighbors.shape[1]
    stats = stations.shape[0]
    radius = (nbrs - 1) // 2
    rounds = int(math.log2(n_elem))
    slots = max(n_col, LANES // cols)
    sizes = (cols, elems, order, nbrs, stats, n_elem, n_col)
    full, width = elems * order, radius * order
    copies = 4 * STEPS + 11 + (n_col - 1) + rounds
    scratch = [pltpu.VMEM((nbrs, order, order), F32)] * elems
    scratch += [pltpu.VMEM((order, nbrs * order), BF16)] * (2 * elems)
    scratch += [
        pltpu.VMEM((elems, cols, order), F32),
        pltpu.VMEM((LANES, order), F32),
        pltpu.VMEM((STEPS + 1, cols, full), F32),
        pltpu.VMEM((2 * cols, full + 2 * width), BF16),
        pltpu.VMEM((STEPS, cols, width), F32),
        pltpu.VMEM((STEPS, cols, width), F32),
        pltpu.VMEM((STEPS + 1, cols, full), F32),
        pltpu.VMEM((cols, full), F32),
        pltpu.VMEM((cols, full), F32),
        pltpu.VMEM((STEPS, cols, width), F32),
        pltpu.VMEM((STEPS, cols, width), F32),
        pltpu.VMEM((STEPS, cols, width), F32),
        pltpu.VMEM((STEPS, cols, width), F32),
        pltpu.VMEM((cols, width), F32),
        pltpu.VMEM((2, cols, width // 2), F32),
        pltpu.VMEM((cols, width // 2), F32),
        pltpu.VMEM((slots, cols, LANES), F32),
        pltpu.VMEM((rounds + 1, cols, slots * cols), F32),
        pltpu.VMEM((rounds + 1, cols, slots * cols), F32),
        pltpu.VMEM((elems, cols, order // 2), F32),
        pltpu.VMEM((elems, cols, order // 2), F32),
        pltpu.SemaphoreType.DMA((elems + 2,)),
        pltpu.SemaphoreType.DMA((copies,)),
        pltpu.SemaphoreType.DMA((copies,)),
    ]
    smem = pl.BlockSpec(memory_space=pltpu.SMEM)
    anywhere = pl.BlockSpec(memory_space=pl.ANY)
    vmem = pl.BlockSpec(memory_space=pltpu.VMEM)
    hess, gram = pl.pallas_call(
        functools.partial(kernel, sizes),
        out_shape=(
            jax.ShapeDtypeStruct((elems, cols, order // 2), F32),
            jax.ShapeDtypeStruct((cols, slots * cols), F32),
        ),
        in_specs=[smem, smem, anywhere, anywhere, anywhere],
        out_specs=(vmem, vmem),
        scratch_shapes=scratch,
        compiler_params=pltpu.CompilerParams(
            collective_id=0, has_side_effects=True, vmem_limit_bytes=56 * 1024 * 1024
        ),
    )(neighbors, stations, probes.transpose(1, 0, 2), jacobian, obs_weights)
    hess, gram = pl.pallas_call(
        hand_over,
        out_shape=(
            jax.ShapeDtypeStruct(hess.shape, F32),
            jax.ShapeDtypeStruct((cols, n_col * cols), F32),
        ),
        in_specs=[vmem, vmem],
        out_specs=(vmem, vmem),
    )(hess, gram)
    return hess.transpose(1, 0, 2), gram


def solution(mesh):
    in_specs = (
        P("col", "elem", None),
        P("sec", "elem", None, None, None),
        P("elem", None),
        P("elem"),
        P("elem", None),
    )
    out_specs = (P("col", "elem", "sec"), P("col", None))
    body = functools.partial(per_device, mesh.shape["elem"], mesh.shape["col"])
    return jax.shard_map(
        body, mesh=mesh, in_specs=in_specs, out_specs=out_specs, check_vma=False
    )
```

```python
import functools
import math

import jax
import jax.numpy as jnp
from jax import lax
from jax.experimental import pallas as pl
from jax.experimental.pallas import tpu as pltpu
from jax.sharding import PartitionSpec as P

STEPS = 2
MESH = pl.DeviceIdType.MESH
F32 = jnp.float32
BF16 = jnp.bfloat16
LANES = 128


def halves(value):
    high = value.astype(BF16)
    low = (value - high.astype(F32)).astype(BF16)
    return high, low


def product(a, b, transposed):
    dims = (((1,), (1 if transposed else 0,)), ((), ()))
    return lax.dot_general(a, b, dims, preferred_element_type=F32)


def product3(stack, high, low, transposed):
    rows = stack.shape[0] // 2
    first = product(stack, high, transposed)
    second = product(stack[:rows], low, transposed)
    return first[:rows] + (first[rows:] + second)


def kernel(
    sizes,
    neighbors,
    stations,
    probes_hbm,
    jacobian_hbm,
    weights_hbm,
    hess_ref,
    gram_ref,
    *scratch,
):
    cols, elems, order, nbrs, stats, n_elem, n_col = sizes
    radius = (nbrs - 1) // 2
    width = radius * order
    half = order // 2
    jac_f32 = scratch[:elems]
    jac_high = scratch[elems : 2 * elems]
    jac_low = scratch[2 * elems : 3 * elems]
    (
        probes_ref, weights_ref, state, field, halo_left, halo_right,
        adjoint, adjoint_in, observed, out_left, out_right, back_left, back_right,
        back_across, out_half, back_half, readings, partial, partial_in, upper, upper_in,
        load_sem, send_sem, recv_sem,
    ) = scratch[3 * elems :]
    section = lax.axis_index("sec")
    column = lax.axis_index("col")
    block = lax.axis_index("elem")
    left = lax.rem(block + n_elem - 1, n_elem)
    right = lax.rem(block + 1, n_elem)
    even = lax.rem(block, 2) == 0
    far = jnp.where(even, left, right)
    other = 1 - section
    first_elem = block * elems
    elem_total = elems * n_elem
    rounds = int(math.log2(n_elem))
    edge = radius + elems
    full = elems * order
    last = STEPS - 1
    LEFT, RIGHT = 0, 1
    neighbour = (left, right)
    halo_in = (halo_left, halo_right)
    out = (out_left, out_right)
    back = (back_left, back_right)
    own = (slice(0, width), slice(full - width, full))
    own_ds = (pl.ds(0, width), pl.ds(full - width, width))
    own_elems = (range(0, radius), range(elems - radius, elems))
    own_span = ((radius, 2 * radius), (edge - radius, edge))

    def by_parity(run):
        @pl.when(even)
        def _():
            run(RIGHT, LEFT)

        @pl.when(jnp.logical_not(even))
        def _():
            run(LEFT, RIGHT)

    probe_load = pltpu.make_async_copy(probes_hbm, probes_ref, load_sem.at[elems])
    probe_load.start()
    jac_loads = [
        pltpu.make_async_copy(jacobian_hbm.at[0, e], jac_f32[e], load_sem.at[e])
        for e in range(elems)
    ]
    for load in jac_loads:
        load.start()
    weights_load = pltpu.make_async_copy(
        weights_hbm, weights_ref.at[pl.ds(0, stats)], load_sem.at[elems + 1]
    )
    weights_load.start()

    barrier = pltpu.get_barrier_semaphore()
    partners = [{"elem": left}, {"elem": right}, {"sec": other}, {"sec": other, "elem": far}]
    partners += [{"col": lax.rem(column + j, n_col)} for j in range(1, n_col)]
    flips = []
    for r in range(rounds):
        bit = 1 << r
        upper_bit = lax.rem(block // bit, 2)
        flips.append({"elem": block + bit - 2 * bit * upper_bit})
    for partner in partners + flips:
        pl.semaphore_signal(barrier, inc=1, device_id=partner, device_id_type=MESH)

    probe_load.wait()

    @pl.when(section == 0)
    def _():
        for e in range(elems):
            state[0, :, e * order : (e + 1) * order] = probes_ref[e]

    pl.semaphore_wait(barrier, len(partners) + len(flips))

    def remote(src, dst, index, target, arrival=None):
        arrival = index if arrival is None else arrival
        return pltpu.make_async_remote_copy(
            src_ref=src, dst_ref=dst, send_sem=send_sem.at[index],
            recv_sem=recv_sem.at[arrival], device_id=target, device_id_type=MESH,
        )

    FORWARD = 4 * STEPS
    BACKWARD, UPPER = FORWARD + 2, FORWARD + 4
    ACROSS, RETURN, GRAM, LOWER, HIGHER, READ = (FORWARD + 6 + i for i in range(6))
    FLIP = READ + n_col - 1

    def halo_copy(t, side):
        return remote(
            state.at[t, :, own_ds[side]], halo_in[1 - side].at[t], 2 * t + side,
            {"elem": neighbour[side]},
        )

    def halo_across(side):
        return remote(
            state.at[STEPS, :, own_ds[side]], halo_in[1 - side].at[0], ACROSS,
            {"sec": other, "elem": neighbour[side]}, side,
        )

    def forward(side):
        return remote(
            state.at[STEPS, :, own_ds[side]], state.at[0, :, own_ds[side]],
            FORWARD + side, {"sec": other},
        )

    def out_copy(t, side):
        return remote(
            out[side].at[t], back[1 - side].at[t], 2 * STEPS + 2 * t + side,
            {"elem": neighbour[side]},
        )

    def out_across(side):
        return remote(
            out[side].at[last], back_across, RETURN, {"sec": other, "elem": neighbour[side]}
        )

    def backward(side):
        return remote(
            adjoint.at[STEPS, :, own_ds[side]], adjoint_in.at[:, own_ds[side]],
            BACKWARD + side, {"sec": other},
        )

    def half_copy(part, side):
        return remote(
            out_half.at[part], back_half, (LOWER, HIGHER)[part],
            {"sec": section if part == 0 else other, "elem": neighbour[side]},
        )

    def up(side):
        rows = pl.ds(own_elems[side].start, radius)
        return remote(upper.at[rows], upper_in.at[rows], UPPER + side, {"sec": other})

    @pl.when(section == 0)
    def _():
        halo_copy(0, LEFT).start()
        halo_copy(0, RIGHT).start()

    def put_field(start, value):
        high, low = halves(value)
        field[:cols, start : start + value.shape[1]] = high
        field[cols:, start : start + value.shape[1]] = low

    def blocks(ref, begin, end):
        return ref[:, begin * order : end * order]

    def gathered(e, low, high):
        return product3(
            blocks(field, low, high), blocks(jac_high[e], low - e, high - e),
            blocks(jac_low[e], low - e, high - e), True,
        )

    def here(e):
        return slice(e * order, (e + 1) * order)

    def split(e, d, lanes):
        target = lax.rem(first_elem + e + d - radius + elem_total, elem_total)
        slot = jnp.int32(0)
        for k in range(1, nbrs):
            slot = jnp.where(neighbors[e, k] == target, jnp.int32(k), slot)
        high, low = halves(jac_f32[e][slot])
        jac_high[e][:, lanes] = high
        jac_low[e][:, lanes] = low

    def inner_tangent(t, e):
        added = gathered(e, max(e, radius), min(e + nbrs, edge))
        state[t + 1, :, here(e)] = state[t, :, here(e)] + added

    @pl.when(section == 0)
    def _():
        put_field(width, state[0])
        for e in range(elems):
            jac_loads[e].wait()
            for d in range(nbrs):
                split(e, d, here(d))
            if e > 0:
                inner_tangent(0, e - 1)
        inner_tangent(0, elems - 1)

    @pl.when(section == 1)
    def _():
        for e in range(elems):
            jac_loads[e].wait()

            def split_one(d, carry, e=e):
                split(e, d, pl.ds(pl.multiple_of(d * order, order), order))
                return carry

            lax.fori_loop(0, nbrs, split_one, 0)

    weights_load.wait()
    weights_ref[stats:, :] = jnp.zeros((weights_ref.shape[0] - stats, order), F32)
    weights_high, weights_low = halves(weights_ref[...])
    lane_ids = lax.broadcasted_iota(jnp.int32, (cols, LANES), 1)
    station_row = jnp.full((cols, LANES), -1, jnp.int32)
    for i in range(stats):
        station_row = jnp.where(lane_ids == i, stations[i], station_row)

    def finish_tangent(t, side, away):
        halo_copy(t, 1 - side).wait_recv()
        put_field(0 if side == LEFT else width + full, halo_in[side][t])
        for e in own_elems[side]:
            span = (e, radius) if side == LEFT else (edge, e + nbrs)
            state[t + 1, :, here(e)] = state[t + 1, :, here(e)] + gathered(e, *span)
        if t < last:
            halo_copy(t + 1, side).start()
        else:

            @pl.when(section == 0)
            def _():
                forward(side).start()
                if away:
                    halo_across(side).start()

    def tangent(t, core, away):
        if t == 0:

            @pl.when(section == 1)
            def _():
                for side in (core, away):
                    forward(side).wait_recv()
                    if side == core:
                        halo_copy(0, core).start()
                    put_field(width + own[side].start, state[0, :, own[side]])
                    begin, end = own_span[side]
                    for e in range(elems):
                        added = gathered(e, max(e, begin), min(e + nbrs, end))
                        if side == away:
                            added = added + (state[1, :, here(e)] + state[0, :, here(e)])
                        state[1, :, here(e)] = added

        finish_tangent(t, core, False)
        finish_tangent(t, away, True)

    for t in range(STEPS):
        if t > 0:
            put_field(width, state[t])
            for e in range(elems):
                inner_tangent(t, e)
        by_parity(functools.partial(tangent, t))

    reading = jnp.zeros((cols, LANES), F32)
    for e in range(elems):
        stack = jnp.concatenate(halves(state[STEPS, :, here(e)]), axis=0)
        read = product3(stack, weights_high, weights_low, True)
        read = jnp.where(station_row == first_elem + e, read, 0.0)
        reading = reading + read
        stack = jnp.concatenate(halves(read), axis=0)
        observed[:, here(e)] = product3(stack, weights_high, weights_low, False)
    for slot in range(n_col, readings.shape[0]):
        readings[slot] = jnp.zeros((cols, LANES), F32)
    readings[column] = reading
    read_copies = [
        remote(
            readings.at[column], readings.at[column], READ + j - 1,
            {"col": lax.rem(column + j, n_col)},
        )
        for j in range(1, n_col)
    ]
    for copy in read_copies:
        copy.start()
    gram_copy = remote(partial.at[rounds], partial_in.at[rounds], GRAM, {"sec": other})

    def project_start():
        for copy in read_copies:
            copy.wait_recv()
        everyone = readings[...].reshape(readings.shape[0] * cols, LANES)
        high, low = halves(everyone)
        stack = jnp.concatenate(halves(readings[column]), axis=0)
        partial[0] = product3(stack, high, low, True)
        flip_copy(0).start()

    def flip_copy(r):
        return remote(partial.at[r], partial_in.at[r], FLIP + r, flips[r])

    def project_finish():
        for r in range(rounds):
            copy = flip_copy(r)
            if r > 0:
                copy.start()
            copy.wait_recv()
            partial[r + 1] = partial[r] + partial_in[r]
            copy.wait_send()
        gram_copy.start()

    @pl.when(section == 0)
    def _():
        project_start()
        project_finish()

    def spread(e, low, high):
        return product3(
            field[:, here(e)], blocks(jac_high[e], low - e, high - e),
            blocks(jac_low[e], low - e, high - e), False,
        )

    def send_out(t, side, away):
        put_field(own[side].start, adjoint[t, :, own[side]])
        ref = out[side]
        if side == LEFT:
            ref[t] = spread(0, 0, radius)
            for e in range(1, radius):
                ref[t, :, e * order :] = ref[t, :, e * order :] + spread(e, e, radius)
        else:
            ref[t] = spread(elems - 1, edge, edge + radius)
            for e in range(elems - radius, elems - 1):
                size = (e + nbrs - edge) * order
                ref[t, :, :size] = ref[t, :, :size] + spread(e, edge, e + nbrs)
        if t == last and away:

            @pl.when(section == 0)
            def _():
                for part in range(2):
                    for j in range(radius):
                        lanes = slice(j * order + part * half, j * order + (part + 1) * half)
                        out_half[part, :, j * half : (j + 1) * half] = ref[t, :, lanes]
                    half_copy(part, side).start()

            @pl.when(section == 1)
            def _():
                out_across(side).start()

        else:
            out_copy(t, side).start()

    def begin_adjoint(core, away):
        for side in (away, core):
            lanes = own[side]

            @pl.when(section == 0)
            def _():
                backward(side).wait_recv()
                total = adjoint_in[:, lanes] + observed[:, lanes]
                if side == away:
                    out_across(1 - side).wait_recv()
                    total = total + back_across[...]
                adjoint[0, :, lanes] = total

            @pl.when(section == 1)
            def _():
                adjoint[0, :, lanes] = observed[:, lanes]

            send_out(0, side, side == away)

    by_parity(begin_adjoint)

    def inner(t, side):
        begin, end = own_span[side]
        lanes = own[side]
        adjoint[t + 1, :, lanes] = adjoint[t, :, lanes]
        for e in range(elems):
            low, high = max(e, begin), min(e + nbrs, end)
            lanes = slice((low - radius) * order, (high - radius) * order)
            adjoint[t + 1, :, lanes] = adjoint[t + 1, :, lanes] + spread(e, low, high)

    def add_back(t, side):
        lanes = own[side]
        out_copy(t, 1 - side).wait_recv()
        adjoint[t + 1, :, lanes] = adjoint[t + 1, :, lanes] + back[side][t]

    def send_up(side):
        for e in own_elems[side]:
            upper[e] = adjoint[STEPS, :, e * order + half : (e + 1) * order]
        up(side).start()

    def lower_half(e):
        return adjoint[STEPS, :, e * order : e * order + half]

    def adjoint_step(t, core, away):
        if t < last:
            for side in (core, away):
                add_back(t, side)
                send_out(t + 1, side, side == away)
        else:
            inner(t, away)

            @pl.when(section == 0)
            def _():
                send_up(away)

            @pl.when(section == 1)
            def _():
                backward(away).start()

            inner(t, core)
            add_back(t, core)

            @pl.when(section == 0)
            def _():
                send_up(core)
                for e in own_elems[core]:
                    hess_ref[e] = lower_half(e)
                half_copy(0, 1 - away).wait_recv()
                for j, e in enumerate(own_elems[away]):
                    hess_ref[e] = lower_half(e) + back_half[:, j * half : (j + 1) * half]

            @pl.when(section == 1)
            def _():
                backward(core).start()

    for t in range(STEPS):
        if t < last:
            inner(t, LEFT)
            inner(t, RIGHT)
        if t == 0:

            @pl.when(section == 1)
            def _():
                project_start()

        by_parity(functools.partial(adjoint_step, t))

    @pl.when(section == 1)
    def _():
        project_finish()

    gram_copy.wait_recv()
    scale = 1.0 / (elem_total * order)
    gram_ref[...] = (partial[rounds] + partial_in[rounds]) * scale

    def close(core, away):
        for t in range(STEPS):
            for side in (core, away):

                @pl.when((section == 0) | (t > 0) | (side == core))
                def _():
                    halo_copy(t, side).wait_send()

                if t < last or side == core:
                    out_copy(t, side).wait_send()

        @pl.when(section == 0)
        def _():
            halo_across(away).wait_send()
            for side in (core, away):
                forward(side).wait_send()
                up(side).wait_send()
            for part in range(2):
                half_copy(part, away).wait_send()

        @pl.when(section == 1)
        def _():
            out_across(away).wait_send()
            for side in (core, away):
                backward(side).wait_send()
                up(side).wait_recv()
            for e in own_elems[core]:
                hess_ref[e] = upper_in[e]
            half_copy(1, 1 - away).wait_recv()
            for j, e in enumerate(own_elems[away]):
                hess_ref[e] = upper_in[e] + back_half[:, j * half : (j + 1) * half]

    by_parity(close)
    gram_copy.wait_send()
    for copy in read_copies:
        copy.wait_send()


def hand_over(hess_ref, gram_ref, hess_out, gram_out):
    hess_out[...] = hess_ref[...]
    gram_out[...] = gram_ref[:, : gram_out.shape[1]]


def per_device(n_elem, n_col, probes, jacobian, neighbors, stations, obs_weights):
    cols, elems, order = probes.shape
    nbrs = neighbors.shape[1]
    stats = stations.shape[0]
    radius = (nbrs - 1) // 2
    rounds = int(math.log2(n_elem))
    slots = max(n_col, LANES // cols)
    sizes = (cols, elems, order, nbrs, stats, n_elem, n_col)
    full, width = elems * order, radius * order
    copies = 4 * STEPS + 11 + (n_col - 1) + rounds
    scratch = [pltpu.VMEM((nbrs, order, order), F32)] * elems
    scratch += [pltpu.VMEM((order, nbrs * order), BF16)] * (2 * elems)
    scratch += [
        pltpu.VMEM((elems, cols, order), F32),
        pltpu.VMEM((LANES, order), F32),
        pltpu.VMEM((STEPS + 1, cols, full), F32),
        pltpu.VMEM((2 * cols, full + 2 * width), BF16),
        pltpu.VMEM((STEPS, cols, width), F32),
        pltpu.VMEM((STEPS, cols, width), F32),
        pltpu.VMEM((STEPS + 1, cols, full), F32),
        pltpu.VMEM((cols, full), F32),
        pltpu.VMEM((cols, full), F32),
        pltpu.VMEM((STEPS, cols, width), F32),
        pltpu.VMEM((STEPS, cols, width), F32),
        pltpu.VMEM((STEPS, cols, width), F32),
        pltpu.VMEM((STEPS, cols, width), F32),
        pltpu.VMEM((cols, width), F32),
        pltpu.VMEM((2, cols, width // 2), F32),
        pltpu.VMEM((cols, width // 2), F32),
        pltpu.VMEM((slots, cols, LANES), F32),
        pltpu.VMEM((rounds + 1, cols, slots * cols), F32),
        pltpu.VMEM((rounds + 1, cols, slots * cols), F32),
        pltpu.VMEM((elems, cols, order // 2), F32),
        pltpu.VMEM((elems, cols, order // 2), F32),
        pltpu.SemaphoreType.DMA((elems + 2,)),
        pltpu.SemaphoreType.DMA((copies,)),
        pltpu.SemaphoreType.DMA((copies,)),
    ]
    smem = pl.BlockSpec(memory_space=pltpu.SMEM)
    anywhere = pl.BlockSpec(memory_space=pl.ANY)
    vmem = pl.BlockSpec(memory_space=pltpu.VMEM)
    hess, gram = pl.pallas_call(
        functools.partial(kernel, sizes),
        out_shape=(
            jax.ShapeDtypeStruct((elems, cols, order // 2), F32),
            jax.ShapeDtypeStruct((cols, slots * cols), F32),
        ),
        in_specs=[smem, smem, anywhere, anywhere, anywhere],
        out_specs=(vmem, vmem),
        scratch_shapes=scratch,
        compiler_params=pltpu.CompilerParams(
            collective_id=0, has_side_effects=True, vmem_limit_bytes=56 * 1024 * 1024
        ),
    )(neighbors, stations, probes.transpose(1, 0, 2), jacobian, obs_weights)
    hess, gram = pl.pallas_call(
        hand_over,
        out_shape=(
            jax.ShapeDtypeStruct(hess.shape, F32),
            jax.ShapeDtypeStruct((cols, n_col * cols), F32),
        ),
        in_specs=[vmem, vmem],
        out_specs=(vmem, vmem),
    )(hess, gram)
    return hess.transpose(1, 0, 2), gram


def solution(mesh):
    in_specs = (
        P("col", "elem", None),
        P("sec", "elem", None, None, None),
        P("elem", None),
        P("elem"),
        P("elem", None),
    )
    out_specs = (P("col", "elem", "sec"), P("col", None))
    body = functools.partial(per_device, mesh.shape["elem"], mesh.shape["col"])
    return jax.shard_map(
        body, mesh=mesh, in_specs=in_specs, out_specs=out_specs, check_vma=False
    )
```

```python
import functools
import math

import jax
import jax.numpy as jnp
from jax import lax
from jax.experimental import pallas as pl
from jax.experimental.pallas import tpu as pltpu
from jax.sharding import PartitionSpec as P

STEPS = 2
MESH = pl.DeviceIdType.MESH
F32 = jnp.float32
BF16 = jnp.bfloat16
LANES = 128


def halves(value):
    high = value.astype(BF16)
    low = (value - high.astype(F32)).astype(BF16)
    return high, low


def product(a, b, transposed):
    dims = (((1,), (1 if transposed else 0,)), ((), ()))
    return lax.dot_general(a, b, dims, preferred_element_type=F32)


def product3(stack, high, low, transposed):
    rows = stack.shape[0] // 2
    first = product(stack, high, transposed)
    second = product(stack[:rows], low, transposed)
    return first[:rows] + (first[rows:] + second)


def kernel(
    sizes,
    neighbors,
    stations,
    probes_hbm,
    jacobian_hbm,
    weights_hbm,
    hess_ref,
    gram_ref,
    *scratch,
):
    cols, elems, order, nbrs, stats, n_elem, n_col = sizes
    radius = (nbrs - 1) // 2
    width = radius * order
    half = order // 2
    jac_f32 = scratch[:elems]
    jac_high = scratch[elems : 2 * elems]
    jac_low = scratch[2 * elems : 3 * elems]
    (
        probes_ref, weights_ref, state, field, halo_left, halo_right,
        adjoint, adjoint_in, observed, out_left, out_right, back_left, back_right,
        back_across, out_half, back_half, readings, partial, partial_in, upper, upper_in,
        load_sem, send_sem, recv_sem,
    ) = scratch[3 * elems :]
    section = lax.axis_index("sec")
    column = lax.axis_index("col")
    block = lax.axis_index("elem")
    left = lax.rem(block + n_elem - 1, n_elem)
    right = lax.rem(block + 1, n_elem)
    even = lax.rem(block, 2) == 0
    far = jnp.where(even, left, right)
    other = 1 - section
    first_elem = block * elems
    elem_total = elems * n_elem
    rounds = int(math.log2(n_elem))
    edge = radius + elems
    full = elems * order
    last = STEPS - 1
    LEFT, RIGHT = 0, 1
    neighbour = (left, right)
    halo_in = (halo_left, halo_right)
    out = (out_left, out_right)
    back = (back_left, back_right)
    own = (slice(0, width), slice(full - width, full))
    own_ds = (pl.ds(0, width), pl.ds(full - width, width))
    own_elems = (range(0, radius), range(elems - radius, elems))
    own_span = ((radius, 2 * radius), (edge - radius, edge))

    def by_parity(run):
        @pl.when(even)
        def _():
            run(RIGHT, LEFT)

        @pl.when(jnp.logical_not(even))
        def _():
            run(LEFT, RIGHT)

    probe_load = pltpu.make_async_copy(probes_hbm, probes_ref, load_sem.at[elems])
    probe_load.start()
    jac_loads = [
        pltpu.make_async_copy(jacobian_hbm.at[0, e], jac_f32[e], load_sem.at[e])
        for e in range(elems)
    ]
    for load in jac_loads:
        load.start()
    weights_load = pltpu.make_async_copy(
        weights_hbm, weights_ref.at[pl.ds(0, stats)], load_sem.at[elems + 1]
    )
    weights_load.start()

    barrier = pltpu.get_barrier_semaphore()
    partners = [{"elem": left}, {"elem": right}, {"sec": other}, {"sec": other, "elem": far}]
    partners += [{"col": lax.rem(column + j, n_col)} for j in range(1, n_col)]
    flips = []
    for r in range(rounds):
        bit = 1 << r
        upper_bit = lax.rem(block // bit, 2)
        flips.append({"elem": block + bit - 2 * bit * upper_bit})
    for partner in partners + flips:
        pl.semaphore_signal(barrier, inc=1, device_id=partner, device_id_type=MESH)

    probe_load.wait()

    @pl.when(section == 0)
    def _():
        for e in range(elems):
            state[0, :, e * order : (e + 1) * order] = probes_ref[e]

    pl.semaphore_wait(barrier, len(partners) + len(flips))

    def remote(src, dst, index, target, arrival=None):
        arrival = index if arrival is None else arrival
        return pltpu.make_async_remote_copy(
            src_ref=src, dst_ref=dst, send_sem=send_sem.at[index],
            recv_sem=recv_sem.at[arrival], device_id=target, device_id_type=MESH,
        )

    FORWARD = 4 * STEPS
    BACKWARD, UPPER = FORWARD + 2, FORWARD + 4
    ACROSS, RETURN, GRAM, LOWER, HIGHER, READ = (FORWARD + 6 + i for i in range(6))
    FLIP = READ + n_col - 1

    def halo_copy(t, side):
        return remote(
            state.at[t, :, own_ds[side]], halo_in[1 - side].at[t], 2 * t + side,
            {"elem": neighbour[side]},
        )

    def halo_across(side):
        return remote(
            state.at[STEPS, :, own_ds[side]], halo_in[1 - side].at[0], ACROSS,
            {"sec": other, "elem": neighbour[side]}, side,
        )

    def forward(side):
        return remote(
            state.at[STEPS, :, own_ds[side]], state.at[0, :, own_ds[side]],
            FORWARD + side, {"sec": other},
        )

    def out_copy(t, side):
        return remote(
            out[side].at[t], back[1 - side].at[t], 2 * STEPS + 2 * t + side,
            {"elem": neighbour[side]},
        )

    def out_across(side):
        return remote(
            out[side].at[last], back_across, RETURN, {"sec": other, "elem": neighbour[side]}
        )

    def backward(side):
        return remote(
            adjoint.at[STEPS, :, own_ds[side]], adjoint_in.at[:, own_ds[side]],
            BACKWARD + side, {"sec": other},
        )

    def half_copy(part, side):
        return remote(
            out_half.at[part], back_half, (LOWER, HIGHER)[part],
            {"sec": section if part == 0 else other, "elem": neighbour[side]},
        )

    def up(side):
        rows = pl.ds(own_elems[side].start, radius)
        return remote(upper.at[rows], upper_in.at[rows], UPPER + side, {"sec": other})

    @pl.when(section == 0)
    def _():
        halo_copy(0, LEFT).start()
        halo_copy(0, RIGHT).start()

    def put_field(start, value):
        high, low = halves(value)
        field[:cols, start : start + value.shape[1]] = high
        field[cols:, start : start + value.shape[1]] = low

    def blocks(ref, begin, end):
        return ref[:, begin * order : end * order]

    def gathered(e, low, high):
        return product3(
            blocks(field, low, high), blocks(jac_high[e], low - e, high - e),
            blocks(jac_low[e], low - e, high - e), True,
        )

    def here(e):
        return slice(e * order, (e + 1) * order)

    def split(e, d, lanes):
        target = lax.rem(first_elem + e + d - radius + elem_total, elem_total)
        slot = jnp.int32(0)
        for k in range(1, nbrs):
            slot = jnp.where(neighbors[e, k] == target, jnp.int32(k), slot)
        high, low = halves(jac_f32[e][slot])
        jac_high[e][:, lanes] = high
        jac_low[e][:, lanes] = low

    def inner_tangent(t, e):
        added = gathered(e, max(e, radius), min(e + nbrs, edge))
        state[t + 1, :, here(e)] = state[t, :, here(e)] + added

    @pl.when(section == 0)
    def _():
        put_field(width, state[0])

    for e in range(elems):
        jac_loads[e].wait()

        def split_one(d, carry, e=e):
            split(e, d, pl.ds(pl.multiple_of(d * order, order), order))
            return carry

        lax.fori_loop(0, nbrs, split_one, 0)

        @pl.when(section == 0)
        def _():
            inner_tangent(0, e)

    weights_load.wait()
    weights_ref[stats:, :] = jnp.zeros((weights_ref.shape[0] - stats, order), F32)
    weights_high, weights_low = halves(weights_ref[...])
    lane_ids = lax.broadcasted_iota(jnp.int32, (cols, LANES), 1)
    station_row = jnp.full((cols, LANES), -1, jnp.int32)
    for i in range(stats):
        station_row = jnp.where(lane_ids == i, stations[i], station_row)

    def finish_tangent(t, side, away):
        halo_copy(t, 1 - side).wait_recv()
        put_field(0 if side == LEFT else width + full, halo_in[side][t])
        for e in own_elems[side]:
            span = (e, radius) if side == LEFT else (edge, e + nbrs)
            state[t + 1, :, here(e)] = state[t + 1, :, here(e)] + gathered(e, *span)
        if t < last:
            halo_copy(t + 1, side).start()
        else:

            @pl.when(section == 0)
            def _():
                forward(side).start()
                if away:
                    halo_across(side).start()

    def tangent(t, core, away):
        if t == 0:

            @pl.when(section == 1)
            def _():
                for side in (core, away):
                    forward(side).wait_recv()
                    if side == core:
                        halo_copy(0, core).start()
                    put_field(width + own[side].start, state[0, :, own[side]])
                    begin, end = own_span[side]
                    for e in range(elems):
                        added = gathered(e, max(e, begin), min(e + nbrs, end))
                        if side == away:
                            added = added + (state[1, :, here(e)] + state[0, :, here(e)])
                        state[1, :, here(e)] = added

        finish_tangent(t, core, False)
        finish_tangent(t, away, True)

    for t in range(STEPS):
        if t > 0:
            put_field(width, state[t])
            for e in range(elems):
                inner_tangent(t, e)
        by_parity(functools.partial(tangent, t))

    reading = jnp.zeros((cols, LANES), F32)
    for e in range(elems):
        stack = jnp.concatenate(halves(state[STEPS, :, here(e)]), axis=0)
        read = product3(stack, weights_high, weights_low, True)
        read = jnp.where(station_row == first_elem + e, read, 0.0)
        reading = reading + read
        stack = jnp.concatenate(halves(read), axis=0)
        observed[:, here(e)] = product3(stack, weights_high, weights_low, False)
    for slot in range(n_col, readings.shape[0]):
        readings[slot] = jnp.zeros((cols, LANES), F32)
    readings[column] = reading
    read_copies = [
        remote(
            readings.at[column], readings.at[column], READ + j - 1,
            {"col": lax.rem(column + j, n_col)},
        )
        for j in range(1, n_col)
    ]
    for copy in read_copies:
        copy.start()
    gram_copy = remote(partial.at[rounds], partial_in.at[rounds], GRAM, {"sec": other})

    def project_start():
        for copy in read_copies:
            copy.wait_recv()
        everyone = readings[...].reshape(readings.shape[0] * cols, LANES)
        high, low = halves(everyone)
        stack = jnp.concatenate(halves(readings[column]), axis=0)
        partial[0] = product3(stack, high, low, True)
        flip_copy(0).start()

    def flip_copy(r):
        return remote(partial.at[r], partial_in.at[r], FLIP + r, flips[r])

    def project_finish():
        for r in range(rounds):
            copy = flip_copy(r)
            if r > 0:
                copy.start()
            copy.wait_recv()
            partial[r + 1] = partial[r] + partial_in[r]
            copy.wait_send()
        gram_copy.start()

    @pl.when(section == 0)
    def _():
        project_start()
        project_finish()

    def spread(e, low, high):
        return product3(
            field[:, here(e)], blocks(jac_high[e], low - e, high - e),
            blocks(jac_low[e], low - e, high - e), False,
        )

    def send_out(t, side, away):
        put_field(own[side].start, adjoint[t, :, own[side]])
        ref = out[side]
        if side == LEFT:
            ref[t] = spread(0, 0, radius)
            for e in range(1, radius):
                ref[t, :, e * order :] = ref[t, :, e * order :] + spread(e, e, radius)
        else:
            ref[t] = spread(elems - 1, edge, edge + radius)
            for e in range(elems - radius, elems - 1):
                size = (e + nbrs - edge) * order
                ref[t, :, :size] = ref[t, :, :size] + spread(e, edge, e + nbrs)
        if t == last and away:

            @pl.when(section == 0)
            def _():
                for part in range(2):
                    for j in range(radius):
                        lanes = slice(j * order + part * half, j * order + (part + 1) * half)
                        out_half[part, :, j * half : (j + 1) * half] = ref[t, :, lanes]
                    half_copy(part, side).start()

            @pl.when(section == 1)
            def _():
                out_across(side).start()

        else:
            out_copy(t, side).start()

    def begin_adjoint(core, away):
        for side in (away, core):
            lanes = own[side]

            @pl.when(section == 0)
            def _():
                backward(side).wait_recv()
                total = adjoint_in[:, lanes] + observed[:, lanes]
                if side == away:
                    out_across(1 - side).wait_recv()
                    total = total + back_across[...]
                adjoint[0, :, lanes] = total

            @pl.when(section == 1)
            def _():
                adjoint[0, :, lanes] = observed[:, lanes]

            send_out(0, side, side == away)

    by_parity(begin_adjoint)

    def inner(t, side):
        begin, end = own_span[side]
        lanes = own[side]
        adjoint[t + 1, :, lanes] = adjoint[t, :, lanes]
        for e in range(elems):
            low, high = max(e, begin), min(e + nbrs, end)
            lanes = slice((low - radius) * order, (high - radius) * order)
            adjoint[t + 1, :, lanes] = adjoint[t + 1, :, lanes] + spread(e, low, high)

    def add_back(t, side):
        lanes = own[side]
        out_copy(t, 1 - side).wait_recv()
        adjoint[t + 1, :, lanes] = adjoint[t + 1, :, lanes] + back[side][t]

    def send_up(side):
        for e in own_elems[side]:
            upper[e] = adjoint[STEPS, :, e * order + half : (e + 1) * order]
        up(side).start()

    def lower_half(e):
        return adjoint[STEPS, :, e * order : e * order + half]

    def adjoint_step(t, core, away):
        if t < last:
            for side in (core, away):
                add_back(t, side)
                send_out(t + 1, side, side == away)
        else:
            inner(t, away)

            @pl.when(section == 0)
            def _():
                send_up(away)

            @pl.when(section == 1)
            def _():
                backward(away).start()

            inner(t, core)
            add_back(t, core)

            @pl.when(section == 0)
            def _():
                send_up(core)
                for e in own_elems[core]:
                    hess_ref[e] = lower_half(e)
                half_copy(0, 1 - away).wait_recv()
                for j, e in enumerate(own_elems[away]):
                    hess_ref[e] = lower_half(e) + back_half[:, j * half : (j + 1) * half]

            @pl.when(section == 1)
            def _():
                backward(core).start()

    for t in range(STEPS):
        if t < last:
            inner(t, LEFT)
            inner(t, RIGHT)
        if t == 0:

            @pl.when(section == 1)
            def _():
                project_start()

        by_parity(functools.partial(adjoint_step, t))

    @pl.when(section == 1)
    def _():
        project_finish()

    gram_copy.wait_recv()
    scale = 1.0 / (elem_total * order)
    gram_ref[...] = (partial[rounds] + partial_in[rounds]) * scale

    def close(core, away):
        for t in range(STEPS):
            for side in (core, away):

                @pl.when((section == 0) | (t > 0) | (side == core))
                def _():
                    halo_copy(t, side).wait_send()

                if t < last or side == core:
                    out_copy(t, side).wait_send()

        @pl.when(section == 0)
        def _():
            halo_across(away).wait_send()
            for side in (core, away):
                forward(side).wait_send()
                up(side).wait_send()
            for part in range(2):
                half_copy(part, away).wait_send()

        @pl.when(section == 1)
        def _():
            out_across(away).wait_send()
            for side in (core, away):
                backward(side).wait_send()
                up(side).wait_recv()
            for e in own_elems[core]:
                hess_ref[e] = upper_in[e]
            half_copy(1, 1 - away).wait_recv()
            for j, e in enumerate(own_elems[away]):
                hess_ref[e] = upper_in[e] + back_half[:, j * half : (j + 1) * half]

    by_parity(close)
    gram_copy.wait_send()
    for copy in read_copies:
        copy.wait_send()


def hand_over(hess_ref, gram_ref, hess_out, gram_out):
    hess_out[...] = hess_ref[...]
    gram_out[...] = gram_ref[:, : gram_out.shape[1]]


def per_device(n_elem, n_col, probes, jacobian, neighbors, stations, obs_weights):
    cols, elems, order = probes.shape
    nbrs = neighbors.shape[1]
    stats = stations.shape[0]
    radius = (nbrs - 1) // 2
    rounds = int(math.log2(n_elem))
    slots = max(n_col, LANES // cols)
    sizes = (cols, elems, order, nbrs, stats, n_elem, n_col)
    full, width = elems * order, radius * order
    copies = 4 * STEPS + 11 + (n_col - 1) + rounds
    scratch = [pltpu.VMEM((nbrs, order, order), F32)] * elems
    scratch += [pltpu.VMEM((order, nbrs * order), BF16)] * (2 * elems)
    scratch += [
        pltpu.VMEM((elems, cols, order), F32),
        pltpu.VMEM((LANES, order), F32),
        pltpu.VMEM((STEPS + 1, cols, full), F32),
        pltpu.VMEM((2 * cols, full + 2 * width), BF16),
        pltpu.VMEM((STEPS, cols, width), F32),
        pltpu.VMEM((STEPS, cols, width), F32),
        pltpu.VMEM((STEPS + 1, cols, full), F32),
        pltpu.VMEM((cols, full), F32),
        pltpu.VMEM((cols, full), F32),
        pltpu.VMEM((STEPS, cols, width), F32),
        pltpu.VMEM((STEPS, cols, width), F32),
        pltpu.VMEM((STEPS, cols, width), F32),
        pltpu.VMEM((STEPS, cols, width), F32),
        pltpu.VMEM((cols, width), F32),
        pltpu.VMEM((2, cols, width // 2), F32),
        pltpu.VMEM((cols, width // 2), F32),
        pltpu.VMEM((slots, cols, LANES), F32),
        pltpu.VMEM((rounds + 1, cols, slots * cols), F32),
        pltpu.VMEM((rounds + 1, cols, slots * cols), F32),
        pltpu.VMEM((elems, cols, order // 2), F32),
        pltpu.VMEM((elems, cols, order // 2), F32),
        pltpu.SemaphoreType.DMA((elems + 2,)),
        pltpu.SemaphoreType.DMA((copies,)),
        pltpu.SemaphoreType.DMA((copies,)),
    ]
    smem = pl.BlockSpec(memory_space=pltpu.SMEM)
    anywhere = pl.BlockSpec(memory_space=pl.ANY)
    vmem = pl.BlockSpec(memory_space=pltpu.VMEM)
    hess, gram = pl.pallas_call(
        functools.partial(kernel, sizes),
        out_shape=(
            jax.ShapeDtypeStruct((elems, cols, order // 2), F32),
            jax.ShapeDtypeStruct((cols, slots * cols), F32),
        ),
        in_specs=[smem, smem, anywhere, anywhere, anywhere],
        out_specs=(vmem, vmem),
        scratch_shapes=scratch,
        compiler_params=pltpu.CompilerParams(
            collective_id=0, has_side_effects=True, vmem_limit_bytes=56 * 1024 * 1024
        ),
    )(neighbors, stations, probes.transpose(1, 0, 2), jacobian, obs_weights)
    hess, gram = pl.pallas_call(
        hand_over,
        out_shape=(
            jax.ShapeDtypeStruct(hess.shape, F32),
            jax.ShapeDtypeStruct((cols, n_col * cols), F32),
        ),
        in_specs=[vmem, vmem],
        out_specs=(vmem, vmem),
    )(hess, gram)
    return hess.transpose(1, 0, 2), gram


def solution(mesh):
    in_specs = (
        P("col", "elem", None),
        P("sec", "elem", None, None, None),
        P("elem", None),
        P("elem"),
        P("elem", None),
    )
    out_specs = (P("col", "elem", "sec"), P("col", None))
    body = functools.partial(per_device, mesh.shape["elem"], mesh.shape["col"])
    return jax.shard_map(
        body, mesh=mesh, in_specs=in_specs, out_specs=out_specs, check_vma=False
    )
```

```python
import functools
import math

import jax
import jax.numpy as jnp
from jax import lax
from jax.experimental import pallas as pl
from jax.experimental.pallas import tpu as pltpu
from jax.sharding import PartitionSpec as P

STEPS = 2
MESH = pl.DeviceIdType.MESH
F32 = jnp.float32
BF16 = jnp.bfloat16
LANES = 128


def halves(value):
    high = value.astype(BF16)
    low = (value - high.astype(F32)).astype(BF16)
    return high, low


def product(a, b, transposed):
    dims = (((1,), (1 if transposed else 0,)), ((), ()))
    return lax.dot_general(a, b, dims, preferred_element_type=F32)


def product3(stack, high, low, transposed):
    rows = stack.shape[0] // 2
    first = product(stack, high, transposed)
    second = product(stack[:rows], low, transposed)
    return first[:rows] + (first[rows:] + second)


def kernel(
    sizes,
    neighbors,
    stations,
    probes_hbm,
    jacobian_hbm,
    weights_hbm,
    hess_ref,
    gram_ref,
    *scratch,
):
    cols, elems, order, nbrs, stats, n_elem, n_col = sizes
    radius = (nbrs - 1) // 2
    width = radius * order
    half = order // 2
    jac_f32 = scratch[:elems]
    jac_high = scratch[elems : 2 * elems]
    jac_low = scratch[2 * elems : 3 * elems]
    (
        probes_ref, weights_ref, state, field, halo_left, halo_right,
        adjoint, adjoint_in, observed, out_left, out_right, back_left, back_right,
        back_across, out_half, back_half, readings, partial, partial_in, upper, upper_in,
        load_sem, send_sem, recv_sem,
    ) = scratch[3 * elems :]
    section = lax.axis_index("sec")
    column = lax.axis_index("col")
    block = lax.axis_index("elem")
    left = lax.rem(block + n_elem - 1, n_elem)
    right = lax.rem(block + 1, n_elem)
    even = lax.rem(block, 2) == 0
    far = jnp.where(even, left, right)
    other = 1 - section
    first_elem = block * elems
    elem_total = elems * n_elem
    rounds = int(math.log2(n_elem))
    edge = radius + elems
    full = elems * order
    last = STEPS - 1
    LEFT, RIGHT = 0, 1
    neighbour = (left, right)
    halo_in = (halo_left, halo_right)
    out = (out_left, out_right)
    back = (back_left, back_right)
    own = (slice(0, width), slice(full - width, full))
    own_ds = (pl.ds(0, width), pl.ds(full - width, width))
    own_elems = (range(0, radius), range(elems - radius, elems))
    own_span = ((radius, 2 * radius), (edge - radius, edge))

    def by_parity(run):
        @pl.when(even)
        def _():
            run(RIGHT, LEFT)

        @pl.when(jnp.logical_not(even))
        def _():
            run(LEFT, RIGHT)

    probe_load = pltpu.make_async_copy(probes_hbm, probes_ref, load_sem.at[elems])
    probe_load.start()
    jac_loads = [
        pltpu.make_async_copy(jacobian_hbm.at[0, e], jac_f32[e], load_sem.at[e])
        for e in range(elems)
    ]
    for load in jac_loads:
        load.start()
    weights_load = pltpu.make_async_copy(
        weights_hbm, weights_ref.at[pl.ds(0, stats)], load_sem.at[elems + 1]
    )
    weights_load.start()

    barrier = pltpu.get_barrier_semaphore()
    partners = [{"elem": left}, {"elem": right}, {"sec": other}, {"sec": other, "elem": far}]
    partners += [{"col": lax.rem(column + j, n_col)} for j in range(1, n_col)]
    flips = []
    for r in range(rounds):
        bit = 1 << r
        upper_bit = lax.rem(block // bit, 2)
        flips.append({"elem": block + bit - 2 * bit * upper_bit})
    for partner in partners + flips:
        pl.semaphore_signal(barrier, inc=1, device_id=partner, device_id_type=MESH)

    probe_load.wait()

    @pl.when(section == 0)
    def _():
        for e in range(elems):
            state[0, :, e * order : (e + 1) * order] = probes_ref[e]

    pl.semaphore_wait(barrier, len(partners) + len(flips))

    def remote(src, dst, index, target, arrival=None):
        arrival = index if arrival is None else arrival
        return pltpu.make_async_remote_copy(
            src_ref=src, dst_ref=dst, send_sem=send_sem.at[index],
            recv_sem=recv_sem.at[arrival], device_id=target, device_id_type=MESH,
        )

    FORWARD = 4 * STEPS
    BACKWARD, UPPER = FORWARD + 2, FORWARD + 4
    ACROSS, RETURN, GRAM, LOWER, HIGHER, READ = (FORWARD + 6 + i for i in range(6))
    FLIP = READ + n_col - 1

    def halo_copy(t, side):
        return remote(
            state.at[t, :, own_ds[side]], halo_in[1 - side].at[t], 2 * t + side,
            {"elem": neighbour[side]},
        )

    def halo_across(side):
        return remote(
            state.at[STEPS, :, own_ds[side]], halo_in[1 - side].at[0], ACROSS,
            {"sec": other, "elem": neighbour[side]}, side,
        )

    def forward(side):
        return remote(
            state.at[STEPS, :, own_ds[side]], state.at[0, :, own_ds[side]],
            FORWARD + side, {"sec": other},
        )

    def out_copy(t, side):
        return remote(
            out[side].at[t], back[1 - side].at[t], 2 * STEPS + 2 * t + side,
            {"elem": neighbour[side]},
        )

    def out_across(side):
        return remote(
            out[side].at[last], back_across, RETURN, {"sec": other, "elem": neighbour[side]}
        )

    def backward(side):
        return remote(
            adjoint.at[STEPS, :, own_ds[side]], adjoint_in.at[:, own_ds[side]],
            BACKWARD + side, {"sec": other},
        )

    def half_copy(part, side):
        return remote(
            out_half.at[part], back_half, (LOWER, HIGHER)[part],
            {"sec": section if part == 0 else other, "elem": neighbour[side]},
        )

    def up(side):
        rows = pl.ds(own_elems[side].start, radius)
        return remote(upper.at[rows], upper_in.at[rows], UPPER + side, {"sec": other})

    @pl.when(section == 0)
    def _():
        halo_copy(0, LEFT).start()
        halo_copy(0, RIGHT).start()

    for e in range(elems):
        jac_loads[e].wait()

        def split_one(d, carry, e=e):
            target = lax.rem(first_elem + e + d - radius + elem_total, elem_total)
            slot = jnp.int32(0)
            for k in range(1, nbrs):
                slot = jnp.where(neighbors[e, k] == target, jnp.int32(k), slot)
            high, low = halves(jac_f32[e][slot])
            lanes = pl.ds(pl.multiple_of(d * order, order), order)
            jac_high[e][:, lanes] = high
            jac_low[e][:, lanes] = low
            return carry

        lax.fori_loop(0, nbrs, split_one, 0)

    weights_load.wait()
    weights_ref[stats:, :] = jnp.zeros((weights_ref.shape[0] - stats, order), F32)
    weights_high, weights_low = halves(weights_ref[...])
    lane_ids = lax.broadcasted_iota(jnp.int32, (cols, LANES), 1)
    station_row = jnp.full((cols, LANES), -1, jnp.int32)
    for i in range(stats):
        station_row = jnp.where(lane_ids == i, stations[i], station_row)

    def put_field(start, value):
        high, low = halves(value)
        field[:cols, start : start + value.shape[1]] = high
        field[cols:, start : start + value.shape[1]] = low

    def blocks(ref, begin, end):
        return ref[:, begin * order : end * order]

    def gathered(e, low, high):
        return product3(
            blocks(field, low, high), blocks(jac_high[e], low - e, high - e),
            blocks(jac_low[e], low - e, high - e), True,
        )

    def here(e):
        return slice(e * order, (e + 1) * order)

    def finish_tangent(t, side, away):
        halo_copy(t, 1 - side).wait_recv()
        put_field(0 if side == LEFT else width + full, halo_in[side][t])
        for e in own_elems[side]:
            span = (e, radius) if side == LEFT else (edge, e + nbrs)
            state[t + 1, :, here(e)] = state[t + 1, :, here(e)] + gathered(e, *span)
        if t < last:
            halo_copy(t + 1, side).start()
        else:

            @pl.when(section == 0)
            def _():
                forward(side).start()
                if away:
                    halo_across(side).start()

    def tangent(t, core, away):
        if t == 0:
            for side in (core, away):

                @pl.when(section == 1)
                def _():
                    forward(side).wait_recv()
                    if side == core:
                        halo_copy(0, core).start()

                put_field(width + own[side].start, state[0, :, own[side]])
                begin, end = own_span[side]
                for e in range(elems):
                    added = gathered(e, max(e, begin), min(e + nbrs, end))
                    if side == away:
                        added = added + (state[1, :, here(e)] + state[0, :, here(e)])
                    state[1, :, here(e)] = added
        finish_tangent(t, core, False)
        finish_tangent(t, away, True)

    for t in range(STEPS):
        if t > 0:
            put_field(width, state[t])
            for e in range(elems):
                added = gathered(e, max(e, radius), min(e + nbrs, edge))
                state[t + 1, :, here(e)] = state[t, :, here(e)] + added
        by_parity(functools.partial(tangent, t))

    reading = jnp.zeros((cols, LANES), F32)
    for e in range(elems):
        stack = jnp.concatenate(halves(state[STEPS, :, here(e)]), axis=0)
        read = product3(stack, weights_high, weights_low, True)
        read = jnp.where(station_row == first_elem + e, read, 0.0)
        reading = reading + read
        stack = jnp.concatenate(halves(read), axis=0)
        observed[:, here(e)] = product3(stack, weights_high, weights_low, False)
    for slot in range(n_col, readings.shape[0]):
        readings[slot] = jnp.zeros((cols, LANES), F32)
    readings[column] = reading
    read_copies = [
        remote(
            readings.at[column], readings.at[column], READ + j - 1,
            {"col": lax.rem(column + j, n_col)},
        )
        for j in range(1, n_col)
    ]
    for copy in read_copies:
        copy.start()
    gram_copy = remote(partial.at[rounds], partial_in.at[rounds], GRAM, {"sec": other})

    def project_start():
        for copy in read_copies:
            copy.wait_recv()
        everyone = readings[...].reshape(readings.shape[0] * cols, LANES)
        high, low = halves(everyone)
        stack = jnp.concatenate(halves(readings[column]), axis=0)
        partial[0] = product3(stack, high, low, True)
        flip_copy(0).start()

    def flip_copy(r):
        return remote(partial.at[r], partial_in.at[r], FLIP + r, flips[r])

    def project_finish():
        for r in range(rounds):
            copy = flip_copy(r)
            if r > 0:
                copy.start()
            copy.wait_recv()
            partial[r + 1] = partial[r] + partial_in[r]
            copy.wait_send()
        gram_copy.start()

    @pl.when(section == 0)
    def _():
        project_start()
        project_finish()

    def spread(e, low, high):
        return product3(
            field[:, here(e)], blocks(jac_high[e], low - e, high - e),
            blocks(jac_low[e], low - e, high - e), False,
        )

    def send_out(t, side, away):
        put_field(own[side].start, adjoint[t, :, own[side]])
        ref = out[side]
        if side == LEFT:
            ref[t] = spread(0, 0, radius)
            for e in range(1, radius):
                ref[t, :, e * order :] = ref[t, :, e * order :] + spread(e, e, radius)
        else:
            ref[t] = spread(elems - 1, edge, edge + radius)
            for e in range(elems - radius, elems - 1):
                size = (e + nbrs - edge) * order
                ref[t, :, :size] = ref[t, :, :size] + spread(e, edge, e + nbrs)
        if t == last and away:

            @pl.when(section == 0)
            def _():
                for part in range(2):
                    for j in range(radius):
                        lanes = slice(j * order + part * half, j * order + (part + 1) * half)
                        out_half[part, :, j * half : (j + 1) * half] = ref[t, :, lanes]
                    half_copy(part, side).start()

            @pl.when(section == 1)
            def _():
                out_across(side).start()

        else:
            out_copy(t, side).start()

    def begin_adjoint(core, away):
        for side in (away, core):
            lanes = own[side]

            @pl.when(section == 0)
            def _():
                backward(side).wait_recv()
                total = adjoint_in[:, lanes] + observed[:, lanes]
                if side == away:
                    out_across(1 - side).wait_recv()
                    total = total + back_across[...]
                adjoint[0, :, lanes] = total

            @pl.when(section == 1)
            def _():
                adjoint[0, :, lanes] = observed[:, lanes]

            send_out(0, side, side == away)

    by_parity(begin_adjoint)

    def inner(t, side):
        begin, end = own_span[side]
        lanes = own[side]
        adjoint[t + 1, :, lanes] = adjoint[t, :, lanes]
        for e in range(elems):
            low, high = max(e, begin), min(e + nbrs, end)
            lanes = slice((low - radius) * order, (high - radius) * order)
            adjoint[t + 1, :, lanes] = adjoint[t + 1, :, lanes] + spread(e, low, high)

    def add_back(t, side):
        lanes = own[side]
        out_copy(t, 1 - side).wait_recv()
        adjoint[t + 1, :, lanes] = adjoint[t + 1, :, lanes] + back[side][t]

    def send_up(side):
        for e in own_elems[side]:
            upper[e] = adjoint[STEPS, :, e * order + half : (e + 1) * order]
        up(side).start()

    def lower_half(e):
        return adjoint[STEPS, :, e * order : e * order + half]

    def adjoint_step(t, core, away):
        if t < last:
            for side in (core, away):
                add_back(t, side)
                send_out(t + 1, side, side == away)
        else:
            inner(t, away)

            @pl.when(section == 0)
            def _():
                send_up(away)

            @pl.when(section == 1)
            def _():
                backward(away).start()

            inner(t, core)
            add_back(t, core)

            @pl.when(section == 0)
            def _():
                send_up(core)
                for e in own_elems[core]:
                    hess_ref[e] = lower_half(e)
                half_copy(0, 1 - away).wait_recv()
                for j, e in enumerate(own_elems[away]):
                    hess_ref[e] = lower_half(e) + back_half[:, j * half : (j + 1) * half]

            @pl.when(section == 1)
            def _():
                backward(core).start()

    for t in range(STEPS):
        if t < last:
            inner(t, LEFT)
            inner(t, RIGHT)
        if t == 0:

            @pl.when(section == 1)
            def _():
                project_start()

        by_parity(functools.partial(adjoint_step, t))

    @pl.when(section == 1)
    def _():
        project_finish()

    gram_copy.wait_recv()
    scale = 1.0 / (elem_total * order)
    gram_ref[...] = (partial[rounds] + partial_in[rounds]) * scale

    def close(core, away):
        for t in range(STEPS):
            for side in (core, away):

                @pl.when((section == 0) | (t > 0) | (side == core))
                def _():
                    halo_copy(t, side).wait_send()

                if t < last or side == core:
                    out_copy(t, side).wait_send()

        @pl.when(section == 0)
        def _():
            halo_across(away).wait_send()
            for side in (core, away):
                forward(side).wait_send()
                up(side).wait_send()
            for part in range(2):
                half_copy(part, away).wait_send()

        @pl.when(section == 1)
        def _():
            out_across(away).wait_send()
            for side in (core, away):
                backward(side).wait_send()
                up(side).wait_recv()
            for e in own_elems[core]:
                hess_ref[e] = upper_in[e]
            half_copy(1, 1 - away).wait_recv()
            for j, e in enumerate(own_elems[away]):
                hess_ref[e] = upper_in[e] + back_half[:, j * half : (j + 1) * half]

    by_parity(close)
    gram_copy.wait_send()
    for copy in read_copies:
        copy.wait_send()


def hand_over(hess_ref, gram_ref, hess_out, gram_out):
    hess_out[...] = hess_ref[...]
    gram_out[...] = gram_ref[:, : gram_out.shape[1]]


def per_device(n_elem, n_col, probes, jacobian, neighbors, stations, obs_weights):
    cols, elems, order = probes.shape
    nbrs = neighbors.shape[1]
    stats = stations.shape[0]
    radius = (nbrs - 1) // 2
    rounds = int(math.log2(n_elem))
    slots = max(n_col, LANES // cols)
    sizes = (cols, elems, order, nbrs, stats, n_elem, n_col)
    full, width = elems * order, radius * order
    copies = 4 * STEPS + 11 + (n_col - 1) + rounds
    scratch = [pltpu.VMEM((nbrs, order, order), F32)] * elems
    scratch += [pltpu.VMEM((order, nbrs * order), BF16)] * (2 * elems)
    scratch += [
        pltpu.VMEM((elems, cols, order), F32),
        pltpu.VMEM((LANES, order), F32),
        pltpu.VMEM((STEPS + 1, cols, full), F32),
        pltpu.VMEM((2 * cols, full + 2 * width), BF16),
        pltpu.VMEM((STEPS, cols, width), F32),
        pltpu.VMEM((STEPS, cols, width), F32),
        pltpu.VMEM((STEPS + 1, cols, full), F32),
        pltpu.VMEM((cols, full), F32),
        pltpu.VMEM((cols, full), F32),
        pltpu.VMEM((STEPS, cols, width), F32),
        pltpu.VMEM((STEPS, cols, width), F32),
        pltpu.VMEM((STEPS, cols, width), F32),
        pltpu.VMEM((STEPS, cols, width), F32),
        pltpu.VMEM((cols, width), F32),
        pltpu.VMEM((2, cols, width // 2), F32),
        pltpu.VMEM((cols, width // 2), F32),
        pltpu.VMEM((slots, cols, LANES), F32),
        pltpu.VMEM((rounds + 1, cols, slots * cols), F32),
        pltpu.VMEM((rounds + 1, cols, slots * cols), F32),
        pltpu.VMEM((elems, cols, order // 2), F32),
        pltpu.VMEM((elems, cols, order // 2), F32),
        pltpu.SemaphoreType.DMA((elems + 2,)),
        pltpu.SemaphoreType.DMA((copies,)),
        pltpu.SemaphoreType.DMA((copies,)),
    ]
    smem = pl.BlockSpec(memory_space=pltpu.SMEM)
    anywhere = pl.BlockSpec(memory_space=pl.ANY)
    vmem = pl.BlockSpec(memory_space=pltpu.VMEM)
    hess, gram = pl.pallas_call(
        functools.partial(kernel, sizes),
        out_shape=(
            jax.ShapeDtypeStruct((elems, cols, order // 2), F32),
            jax.ShapeDtypeStruct((cols, slots * cols), F32),
        ),
        in_specs=[smem, smem, anywhere, anywhere, anywhere],
        out_specs=(vmem, vmem),
        scratch_shapes=scratch,
        compiler_params=pltpu.CompilerParams(
            collective_id=0, has_side_effects=True, vmem_limit_bytes=56 * 1024 * 1024
        ),
    )(neighbors, stations, probes.transpose(1, 0, 2), jacobian, obs_weights)
    hess, gram = pl.pallas_call(
        hand_over,
        out_shape=(
            jax.ShapeDtypeStruct(hess.shape, F32),
            jax.ShapeDtypeStruct((cols, n_col * cols), F32),
        ),
        in_specs=[vmem, vmem],
        out_specs=(vmem, vmem),
    )(hess, gram)
    return hess.transpose(1, 0, 2), gram


def solution(mesh):
    in_specs = (
        P("col", "elem", None),
        P("sec", "elem", None, None, None),
        P("elem", None),
        P("elem"),
        P("elem", None),
    )
    out_specs = (P("col", "elem", "sec"), P("col", None))
    body = functools.partial(per_device, mesh.shape["elem"], mesh.shape["col"])
    return jax.shard_map(
        body, mesh=mesh, in_specs=in_specs, out_specs=out_specs, check_vma=False
    )
```
